32 devices in a mesh: dp: 8 (over z, x), tensor: 4 (over y, core).
Axes of the slice: x: 2, y: 2, z: 4, core: 2. Of those that a mesh axis runs over, the one named last changes fastest.
Arguments:
- inputs: bfloat16 [8, 64, 64, 1280], P('dp', 'tensor'), may hold values from -6 to 6
- cotangent: bfloat16 [8, 64, 64, 1280], P('dp', 'tensor'), may hold values from -6 to 6
- teacher: bfloat16 [8, 64, 64, 1280], P('dp', 'tensor'), may hold values from -6 to 6
- qkv_weight: bfloat16 [3, 1280, 1280], P(None, 'dp', 'tensor'), may hold values from -0.15625 to 0.15625
- proj_weight: bfloat16 [1280, 1280], P('tensor', 'dp'), may hold values from -1 to 1
- up_weight: bfloat16 [1280, 5120], P('dp', 'tensor'), may hold values from -0.15625 to 0.15625
- down_weight: bfloat16 [5120, 1280], P('tensor', 'dp'), may hold values from -0.078125 to 0.078125
- qv_bias: bfloat16 [2, 1280], P(None, 'tensor'), may hold values from -3 to 3
- up_bias: bfloat16 [5120], P('tensor'), may hold values from -3 to 3
- norm_gains: bfloat16 [2, 1280], replicated, may hold values from 0.5 to 1.5
- norm_shifts: bfloat16 [2, 1280], replicated, may hold values from -3 to 3
- out_biases: bfloat16 [2, 1280], replicated, may hold values from -3 to 3
- rel_tables: bfloat16 [2, 27, 80], replicated, may hold values from -0.625 to 0.625
Outputs:
- output: bfloat16 [8, 64, 64, 1280], P('dp', 'tensor')
- input_grad: float32 [8, 64, 64, 1280], P('dp', 'tensor')
- loss: float32 [], replicated
- qkv_weight_grad: float32 [3, 1280, 1280], P(None, 'dp', 'tensor')
- proj_weight_grad: float32 [1280, 1280], P('tensor', 'dp')
- up_weight_grad: float32 [1280, 5120], P('dp', 'tensor')
- down_weight_grad: float32 [5120, 1280], P('tensor', 'dp')
- qv_bias_grad: float32 [2, 1280], P(None, 'tensor')
- up_bias_grad: float32 [5120], P('tensor')
- norm_gains_grad: float32 [2, 1280], replicated
- norm_shifts_grad: float32 [2, 1280], replicated
- out_biases_grad: float32 [2, 1280], replicated
- rel_tables_grad: float32 [2, 27, 80], replicated
The draws below stay inside these ranges and needn't reach their ends.
All inputs are finite; a program needn't handle non-finite values.
Results may differ from the reference program's by a relative error of at most 0.013.
Values may be sent and summed in bfloat16 or wider, within the bound.
A program may use at most 256 MiB of HBM per device.

```python
from functools import partial
import jax
import jax.numpy as jnp
from jax import lax

D = 1280
HEADS = 16
HEAD_DIM = 80
MLP = 5120
GRID = 64
WIN = 14
PGRID = 70
NWIN = 5
IMAGES = 8
TOKENS = 32768


def block_levels(key, dims, shards, least, largest):
    loudness = 1.0
    for dim, shards_of in shards:
        draws = jax.random.uniform(jax.random.fold_in(jax.random.fold_in(key, 6), dim), (shards_of,), jnp.float32, least / len(shards), largest / len(shards))
        loudness = loudness * jnp.repeat(jnp.exp(draws), dims[dim] // shards_of).reshape((-1,) + (1,) * (len(dims) - 1 - dim))
    return loudness


def gaussian(key, shape, deviation, reach, split=(), held_as=jnp.bfloat16):
    drawn = deviation * jax.random.normal(key, shape, jnp.float32)
    if split:
        drawn = drawn * block_levels(key, shape, split, -0.22, 0.18)
    return jnp.clip(drawn, -reach, reach).astype(held_as)


def setup_inputs(seed: int = 0) -> dict:
    keys = jax.random.split(jax.random.key(seed), 14)
    inputs = gaussian(keys[0], (IMAGES, GRID, GRID, D), 1.0, 6.0, ((0, 8), (1, 4)))
    cotangent = gaussian(keys[1], (IMAGES, GRID, GRID, D), 1.0, 6.0, ((0, 8), (1, 4)))
    teacher = gaussian(keys[2], (IMAGES, GRID, GRID, D), 1.0, 6.0, ((0, 8), (1, 4)))
    qkv_weight = gaussian(keys[3], (3, D, D), D ** -0.5, 0.15625, ((1, 8), (2, 4)))
    proj_weight = gaussian(keys[4], (D, D), (D // 32) ** -0.5, 1.0, ((0, 4), (1, 8)))
    up_weight = gaussian(keys[5], (D, MLP), D ** -0.5, 0.15625, ((0, 8), (1, 4)))
    down_weight = gaussian(keys[6], (MLP, D), MLP ** -0.5, 0.078125, ((0, 4), (1, 8)))
    qv_bias = gaussian(keys[7], (2, D), 0.5, 3.0, ((1, 4),))
    up_bias = gaussian(keys[8], (MLP,), 0.5, 3.0, ((0, 4),))
    norm_gains = jnp.clip(1.0 + 0.1 * jax.random.normal(keys[9], (2, D), jnp.float32), 0.5, 1.5).astype(jnp.bfloat16)
    norm_shifts = gaussian(keys[10], (2, D), 0.5, 3.0)
    out_biases = gaussian(keys[11], (2, D), 0.5, 3.0)
    rel_tables = gaussian(keys[12], (2, 2 * WIN - 1, HEAD_DIM), HEAD_DIM ** -0.5, 0.625)
    return dict(inputs=inputs, cotangent=cotangent, teacher=teacher, qkv_weight=qkv_weight, proj_weight=proj_weight, up_weight=up_weight, down_weight=down_weight, qv_bias=qv_bias, up_bias=up_bias, norm_gains=norm_gains, norm_shifts=norm_shifts, out_biases=out_biases, rel_tables=rel_tables)


highest = lax.Precision.HIGHEST

@jax.custom_vjp
def low(v):
    return lax.optimization_barrier(v.astype(jnp.bfloat16)).astype(jnp.float32)

@jax.custom_vjp
def low_back(v):
    return v

def low_keep(v):
    return (low(v), None)

def low_pass(kept, grad):
    return (grad,)

def back_keep(v):
    return (v, None)

def back_low(kept, grad):
    return (low(grad),)
low.defvjp(low_keep, low_pass)
low_back.defvjp(back_keep, back_low)

def layer_norm(values, gain_vector, shift_vector):
    average = lax.optimization_barrier(jnp.mean(values, axis=-1, keepdims=True))
    centred = values - average
    variance = lax.optimization_barrier(jnp.mean(centred * centred, axis=-1, keepdims=True))
    return centred * lax.rsqrt(variance + 1e-06) * gain_vector + shift_vector

def offset_tables(window):
    position = jnp.arange(window * window)
    across = jnp.arange(window)
    ranks = jnp.arange(2 * window - 1)
    high_sel = (position[:, None, None] // window - across[None, :, None] + window - 1 == ranks[None, None, :]).astype(jnp.float32)
    wide_sel = (position[:, None, None] % window - across[None, :, None] + window - 1 == ranks[None, None, :]).astype(jnp.float32)
    return (high_sel, wide_sel)

def to_windows(grid_values):
    extra = PGRID - GRID
    padded = jnp.pad(grid_values, ((0, extra), (0, extra), (0, 0)))
    channels = grid_values.shape[-1]
    shaped = padded.reshape(NWIN, WIN, NWIN, WIN, channels).transpose(0, 2, 1, 3, 4)
    return shaped.reshape(NWIN, NWIN, WIN * WIN, channels)

def from_windows(windowed):
    channels = windowed.shape[-1]
    shaped = windowed.reshape(NWIN, NWIN, WIN, WIN, channels).transpose(0, 2, 1, 3, 4)
    return shaped.reshape(PGRID, PGRID, channels)[:GRID, :GRID]

def window_row(block_parts, tables, selectors):
    queries, key_rows, value_rows = block_parts
    table_high, table_wide = tables
    high_sel, wide_sel = selectors
    raw = low_back(jnp.einsum('wqhc,wkhc->whqk', queries, key_rows, precision=highest) * HEAD_DIM ** (-0.5))
    along_high = jnp.einsum('wqhc,rc->wqhr', queries, table_high, precision=highest)
    along_wide = jnp.einsum('wqhc,rc->wqhr', queries, table_wide, precision=highest)
    bias_high = jnp.einsum('wqhr,qkr->whqk', along_high, high_sel, precision=highest)
    bias_wide = jnp.einsum('wqhr,qkr->whqk', along_wide, wide_sel, precision=highest)
    shaped = raw.reshape(raw.shape[:3] + (WIN, WIN)) + bias_high[..., :, None] + bias_wide[..., None, :]
    scores = shaped.reshape(raw.shape)
    probs_low = low(jax.nn.softmax(scores, axis=-1))
    attended = jnp.einsum('whqk,wkhc->wqhc', probs_low, value_rows, precision=highest)
    return low(low_back(attended))

def forward(inputs, params, teacher):
    qkv_w, proj_w, up_w, down_w, qv_b, up_b, gains, shifts, out_b, tables = params
    selectors = offset_tables(WIN)
    head_shape = (NWIN, NWIN, WIN * WIN, HEADS, HEAD_DIM)

    def image_step(loss_total, pair):
        image, target = pair
        normed = low(layer_norm(image, gains[0], shifts[0]))
        windows = to_windows(normed)
        query_pre = low_back(jnp.einsum('abpd,dc->abpc', windows, qkv_w[0], precision=highest))
        key_pre = low_back(jnp.einsum('abpd,dc->abpc', windows, qkv_w[1], precision=highest))
        value_pre = low_back(jnp.einsum('abpd,dc->abpc', windows, qkv_w[2], precision=highest))
        queries = low(query_pre + qv_b[0]).reshape(head_shape)
        key_rows = low(key_pre).reshape(head_shape)
        value_rows = low(value_pre + qv_b[1]).reshape(head_shape)
        row_fn = jax.checkpoint(partial(window_row, tables=(tables[0], tables[1]), selectors=selectors))
        attended = lax.map(row_fn, (queries, key_rows, value_rows))
        grid_out = from_windows(attended.reshape(NWIN, NWIN, WIN * WIN, D))
        branch = low_back(jnp.einsum('xyc,cd->xyd', grid_out, proj_w, precision=highest)) + out_b[0]
        middle = image + branch
        normed_two = low(layer_norm(middle, gains[1], shifts[1]))
        hidden = low_back(jnp.einsum('xyd,dm->xym', normed_two, up_w, precision=highest)) + up_b
        active = low(jax.nn.gelu(hidden, approximate=False))
        result = middle + low_back(jnp.einsum('xym,md->xyd', active, down_w, precision=highest)) + out_b[1]
        mismatch = result - target
        return (loss_total + jnp.sum(mismatch * mismatch), result)
    loss_total, results = lax.scan(jax.checkpoint(image_step), jnp.zeros((), jnp.float32), (inputs, teacher))
    return (results, loss_total / (TOKENS * D))

def reference(inputs, cotangent, teacher, qkv_weight, proj_weight, up_weight, down_weight, qv_bias, up_bias, norm_gains, norm_shifts, out_biases, rel_tables):
    params = tuple((array.astype(jnp.float32) for array in (qkv_weight, proj_weight, up_weight, down_weight, qv_bias, up_bias, norm_gains, norm_shifts, out_biases, rel_tables)))
    inputs_wide = inputs.astype(jnp.float32)
    teacher_wide = teacher.astype(jnp.float32)

    def objective(image_values, param_values):
        return forward(image_values, param_values, teacher_wide)
    (results, loss), pullback = jax.vjp(objective, inputs_wide, params)
    input_grad, grads = pullback((cotangent.astype(jnp.float32), jnp.asarray(TOKENS * D / 2.0, jnp.float32)))
    return (results.astype(jnp.bfloat16), input_grad, loss, grads[0], grads[1], grads[2], grads[3], grads[4], grads[5], grads[6], grads[7], grads[8], grads[9])
```

```python
from functools import partial

import jax
import jax.numpy as jnp
import numpy as np
from jax import lax
from jax.experimental import pallas as pl
from jax.experimental.pallas import tpu as pltpu
from jax.sharding import PartitionSpec as P

D = 1280
HEAD_DIM = 80
GRID = 64
WIN = 14
PGRID = 70
NWIN = 5


highest = lax.Precision.HIGHEST


def layer_norm(values, gain_vector, shift_vector):
    average = jnp.mean(values, axis=-1, keepdims=True)
    centred = values - average
    variance = jnp.mean(centred * centred, axis=-1, keepdims=True)
    return centred * lax.rsqrt(variance + 1e-06) * gain_vector + shift_vector


def exact_gelu(values):
    return jax.nn.gelu(values, approximate=False)


def offset_tables(window):
    position = jnp.arange(window * window)
    across = jnp.arange(window)
    ranks = jnp.arange(2 * window - 1)
    high_sel = (
        position[:, None, None] // window - across[None, :, None] + window - 1
        == ranks[None, None, :]
    ).astype(jnp.float32)
    wide_sel = (
        position[:, None, None] % window - across[None, :, None] + window - 1
        == ranks[None, None, :]
    ).astype(jnp.float32)
    return (high_sel, wide_sel)


def to_windows(grid_values):
    extra = PGRID - GRID
    padded = jnp.pad(grid_values, ((0, extra), (0, extra), (0, 0)))
    channels = grid_values.shape[-1]
    shaped = padded.reshape(NWIN, WIN, NWIN, WIN, channels).transpose(0, 2, 1, 3, 4)
    return shaped.reshape(NWIN, NWIN, WIN * WIN, channels)


def from_windows(windowed):
    channels = windowed.shape[-1]
    shaped = windowed.reshape(NWIN, NWIN, WIN, WIN, channels).transpose(0, 2, 1, 3, 4)
    return shaped.reshape(PGRID, PGRID, channels)[:GRID, :GRID]


def score_block(queries, key_rows, tables, selectors):
    table_high, table_wide = tables
    high_sel, wide_sel = selectors
    raw = jnp.einsum(
        "wqhc,wkhc->whqk", queries, key_rows, preferred_element_type=jnp.float32
    ) * HEAD_DIM ** (-0.5)
    along_high = jnp.einsum(
        "wqhc,rc->wqhr", queries, table_high, preferred_element_type=jnp.float32
    )
    along_wide = jnp.einsum(
        "wqhc,rc->wqhr", queries, table_wide, preferred_element_type=jnp.float32
    )
    bias_high = jnp.einsum("wqhr,qkr->whqk", along_high, high_sel, precision=highest)
    bias_wide = jnp.einsum("wqhr,qkr->whqk", along_wide, wide_sel, precision=highest)
    shaped = (
        raw.reshape(raw.shape[:3] + (WIN, WIN)) + bias_high[..., :, None] + bias_wide[..., None, :]
    )
    return shaped.reshape(raw.shape)


def attend_row(block_parts, tables, selectors):
    queries, key_rows, value_rows = block_parts
    scores = score_block(queries, key_rows, tables, selectors)
    row_max = jnp.max(scores, axis=-1, keepdims=True)
    shifted = jnp.exp(scores - row_max)
    row_total = jnp.sum(shifted, axis=-1, keepdims=True)
    probs_low = (shifted / row_total).astype(jnp.bfloat16)
    attended = jnp.einsum(
        "whqk,wkhc->wqhc", probs_low, value_rows, preferred_element_type=jnp.float32
    )
    return (attended.astype(jnp.bfloat16), (row_max + jnp.log(row_total))[..., 0])


def attend_back(block_parts, tables, selectors):
    queries, key_rows, value_rows, attended_grad, log_total = block_parts
    high_sel, wide_sel = selectors
    scores = score_block(queries, key_rows, tables, selectors)
    probs = jnp.exp(scores - log_total[..., None])
    probs_grad = jnp.einsum(
        "wqhc,wkhc->whqk", attended_grad, value_rows, preferred_element_type=jnp.float32
    )
    value_grad = jnp.einsum(
        "whqk,wqhc->wkhc",
        probs.astype(jnp.bfloat16),
        attended_grad,
        preferred_element_type=jnp.float32,
    )
    scores_grad = probs * (probs_grad - jnp.sum(probs * probs_grad, axis=-1, keepdims=True))
    scores_low = scores_grad.astype(jnp.bfloat16)
    query_grad = jnp.einsum(
        "whqk,wkhc->wqhc", scores_low, key_rows, preferred_element_type=jnp.float32
    ) * HEAD_DIM ** (-0.5)
    key_grad = jnp.einsum(
        "whqk,wqhc->wkhc", scores_low, queries, preferred_element_type=jnp.float32
    ) * HEAD_DIM ** (-0.5)
    shaped = scores_grad.reshape(scores_grad.shape[:3] + (WIN, WIN))
    rank_high = jnp.einsum("whqa,qar->wqhr", jnp.sum(shaped, axis=-1), high_sel, precision=highest)
    rank_wide = jnp.einsum("whqb,qbr->wqhr", jnp.sum(shaped, axis=-2), wide_sel, precision=highest)
    table_high = tables[0].astype(jnp.float32)
    table_wide = tables[1].astype(jnp.float32)
    query_grad = query_grad + jnp.einsum("wqhr,rc->wqhc", rank_high, table_high, precision=highest)
    query_grad = query_grad + jnp.einsum("wqhr,rc->wqhc", rank_wide, table_wide, precision=highest)
    query_wide = queries.astype(jnp.float32)
    table_grad = jnp.stack(
        [
            jnp.einsum("wqhr,wqhc->rc", rank_high, query_wide, precision=highest),
            jnp.einsum("wqhr,wqhc->rc", rank_wide, query_wide, precision=highest),
        ]
    )
    return (query_grad, key_grad, value_grad, table_grad)


def general_shards(
    inputs,
    cotangent,
    teacher,
    qkv_weight,
    proj_weight,
    up_weight,
    down_weight,
    qv_bias,
    up_bias,
    norm_gains,
    norm_shifts,
    out_biases,
    rel_tables,
):
    qkv_full, proj_full, up_full, down_full = (
        lax.all_gather(qkv_weight, "dp", axis=1, tiled=True),
        lax.all_gather(proj_weight, "dp", axis=1, tiled=True),
        lax.all_gather(up_weight, "dp", axis=0, tiled=True),
        lax.all_gather(down_weight, "dp", axis=1, tiled=True),
    )
    up_matrix, down_matrix, up_bias_all = (up_full, down_full, up_bias)
    images, row_count = (inputs.shape[0], inputs.shape[1])
    local_width = qkv_full.shape[2]
    head_count = local_width // HEAD_DIM
    head_shape = (NWIN, NWIN, WIN * WIN, head_count, HEAD_DIM)
    selectors = offset_tables(WIN)
    tables = (rel_tables[0], rel_tables[1])
    gains_wide = norm_gains.astype(jnp.float32)
    shifts_wide = norm_shifts.astype(jnp.float32)
    source = inputs[0].astype(jnp.float32)
    normed = layer_norm(source, gains_wide[0], shifts_wide[0]).astype(jnp.bfloat16)
    gathered = lax.all_gather(normed, "tensor", axis=0, tiled=True)
    windows = to_windows(gathered)
    projected = jnp.einsum("abpd,sdc->sabpc", windows, qkv_full, preferred_element_type=jnp.float32)
    queries = (projected[0] + qv_bias[0]).astype(jnp.bfloat16).reshape(head_shape)
    key_rows = projected[1].astype(jnp.bfloat16).reshape(head_shape)
    value_rows = (projected[2] + qv_bias[1]).astype(jnp.bfloat16).reshape(head_shape)
    attended, log_totals = lax.map(
        partial(attend_row, tables=tables, selectors=selectors), (queries, key_rows, value_rows)
    )
    grid_out = from_windows(attended.reshape(NWIN, NWIN, WIN * WIN, local_width))
    row_piece = grid_out
    attn_branch = lax.psum_scatter(
        jnp.einsum("xyc,cd->xyd", row_piece, proj_full, preferred_element_type=jnp.float32).astype(
            jnp.bfloat16
        ),
        "tensor",
        scatter_dimension=0,
        tiled=True,
    ).astype(jnp.float32)
    middle = source + attn_branch + out_biases[0].astype(jnp.float32)
    normed_two = layer_norm(middle, gains_wide[1], shifts_wide[1]).astype(jnp.bfloat16)
    mlp_input = lax.all_gather(normed_two, "tensor", axis=0, tiled=True)
    hidden = (
        jnp.einsum("xyd,dm->xym", mlp_input, up_matrix, preferred_element_type=jnp.float32)
        + up_bias_all
    )
    active = exact_gelu(hidden).astype(jnp.bfloat16)
    row_piece = active
    mlp_branch = lax.psum_scatter(
        jnp.einsum(
            "xym,md->xyd", row_piece, down_matrix, preferred_element_type=jnp.float32
        ).astype(jnp.bfloat16),
        "tensor",
        scatter_dimension=0,
        tiled=True,
    ).astype(jnp.float32)
    result = middle + mlp_branch + out_biases[1].astype(jnp.float32)
    mismatch = result - teacher[0].astype(jnp.float32)
    loss_total = jnp.sum(mismatch * mismatch)
    outputs = [result.astype(jnp.bfloat16)]
    result_grad = cotangent[0].astype(jnp.float32) + mismatch
    result_low = result_grad.astype(jnp.bfloat16)
    grad_rows = lax.all_gather(result_low, "tensor", axis=0, tiled=True)
    down_acc = jnp.einsum("xym,xyd->md", active, grad_rows, preferred_element_type=jnp.float32)
    active_grad = jnp.einsum(
        "xyd,md->xym", grad_rows, down_matrix, preferred_element_type=jnp.float32
    )
    gelu_value, gelu_back = jax.vjp(exact_gelu, hidden)
    hidden_grad = gelu_back(active_grad)[0]
    up_bias_acc = jnp.sum(hidden_grad, axis=(0, 1))
    hidden_low = hidden_grad.astype(jnp.bfloat16)
    up_acc = jnp.einsum("xyd,xym->dm", mlp_input, hidden_low, preferred_element_type=jnp.float32)
    row_piece = hidden_low
    second_grad = lax.psum_scatter(
        jnp.einsum("xym,dm->xyd", row_piece, up_matrix, preferred_element_type=jnp.float32).astype(
            jnp.bfloat16
        ),
        "tensor",
        scatter_dimension=0,
        tiled=True,
    ).astype(jnp.float32)
    second_value, second_back = jax.vjp(layer_norm, middle, gains_wide[1], shifts_wide[1])
    middle_part, second_gain, second_shift = second_back(second_grad)
    middle_grad = result_grad + middle_part
    out_bias_acc = jnp.stack([jnp.sum(middle_grad, axis=(0, 1)), jnp.sum(result_grad, axis=(0, 1))])
    middle_low = middle_grad.astype(jnp.bfloat16)
    gathered_grad = lax.all_gather(middle_low, "tensor", axis=0, tiled=True)
    proj_acc = jnp.einsum(
        "xyc,xyd->cd", grid_out, gathered_grad, preferred_element_type=jnp.float32
    )
    attended_grad = jnp.einsum(
        "xyd,cd->xyc", gathered_grad, proj_full, preferred_element_type=jnp.float32
    ).astype(jnp.bfloat16)
    grad_windows = to_windows(attended_grad).reshape(head_shape)
    query_grad, key_grad, value_grad, table_parts = lax.map(
        partial(attend_back, tables=tables, selectors=selectors),
        (queries, key_rows, value_rows, grad_windows, log_totals),
    )
    table_acc = jnp.sum(table_parts, axis=0)
    query_flat = query_grad.reshape(NWIN, NWIN, WIN * WIN, local_width)
    key_flat = key_grad.reshape(NWIN, NWIN, WIN * WIN, local_width)
    value_flat = value_grad.reshape(NWIN, NWIN, WIN * WIN, local_width)
    qv_acc = jnp.stack([jnp.sum(query_flat, axis=(0, 1, 2)), jnp.sum(value_flat, axis=(0, 1, 2))])
    stacked = jnp.stack([query_flat, key_flat, value_flat]).astype(jnp.bfloat16)
    qkv_acc = jnp.einsum("abpd,sabpc->sdc", windows, stacked, preferred_element_type=jnp.float32)
    normed_back = jnp.einsum(
        "sabpc,sdc->abpd", stacked, qkv_full, preferred_element_type=jnp.float32
    )
    first_grad = lax.psum_scatter(
        from_windows(normed_back).astype(jnp.bfloat16), "tensor", scatter_dimension=0, tiled=True
    ).astype(jnp.float32)
    first_value, first_back = jax.vjp(layer_norm, source, gains_wide[0], shifts_wide[0])
    source_part, first_gain, first_shift = first_back(first_grad)
    gain_acc = jnp.stack([first_gain, second_gain])
    shift_acc = jnp.stack([first_shift, second_shift])
    input_grads = [middle_grad + source_part]
    qkv_grad, proj_grad, up_grad, down_grad = (
        lax.psum_scatter(
            qkv_acc.astype(jnp.bfloat16), "dp", scatter_dimension=1, tiled=True
        ).astype(jnp.float32),
        lax.psum_scatter(
            proj_acc.astype(jnp.bfloat16), "dp", scatter_dimension=1, tiled=True
        ).astype(jnp.float32),
        lax.psum_scatter(up_acc.astype(jnp.bfloat16), "dp", scatter_dimension=0, tiled=True).astype(
            jnp.float32
        ),
        lax.psum_scatter(
            down_acc.astype(jnp.bfloat16), "dp", scatter_dimension=1, tiled=True
        ).astype(jnp.float32),
    )
    qv_grad, up_bias_grad = lax.psum((qv_acc, up_bias_acc), "dp")
    gains_grad, shifts_grad, out_grad, table_grad, loss_sum = lax.psum(
        (gain_acc, shift_acc, out_bias_acc, table_acc, loss_total), ("dp", "tensor")
    )
    element_count = images * row_count * GRID * D * lax.axis_size("dp") * lax.axis_size("tensor")
    loss = loss_sum / element_count
    return (
        jnp.stack(outputs),
        jnp.stack(input_grads),
        loss,
        qkv_grad,
        proj_grad,
        up_grad,
        down_grad,
        qv_grad,
        up_bias_grad,
        gains_grad,
        shifts_grad,
        out_grad,
        table_grad,
    )


SIDE = 16
GROUP = 4
KEYS = WIN * SIDE
SLABS = ((0, 128), (0, 256), (128, 256), (128, 384))
SCALE = HEAD_DIM ** (-0.5)
LOG2E = 1.4426950408889634
NT = (((1,), (1,)), ((), ()))
TN = (((0,), (0,)), ((), ()))
NN = (((1,), (0,)), ((), ()))


def dot(a, b, dims):
    return lax.dot_general(a, b, dims, preferred_element_type=jnp.float32)


def bias_tables(rel_tables):
    tables = rel_tables.astype(jnp.bfloat16)

    def place(rows):
        padded = jnp.pad(rows, ((0, 5), (0, 0)))
        eye = jnp.eye(GROUP, dtype=jnp.bfloat16)
        spread = eye[:, None, :, None] * padded[None, :, None, :]
        return spread.reshape(GROUP * 32, GROUP * HEAD_DIM)

    forward = jnp.concatenate([place(tables[0][::-1]), place(tables[1][::-1])])
    backward = jnp.concatenate([place(tables[0][::-1]), place(tables[1])])
    lanes = ((0, 0), (0, 64))
    return jnp.pad(forward, lanes), jnp.pad(backward, lanes)


def selectors():
    key = np.arange(KEYS)
    high, wide = key // SIDE, key % SIDE
    fwd = np.zeros((GROUP, KEYS, 128), np.float32)
    bwd = np.zeros((GROUP, KEYS, 128), np.float32)
    real = wide < WIN
    for head in range(GROUP):
        for j in range(KEYS):
            if real[j]:
                fwd[head, j, 32 * head + high[j]] = 1.0
                fwd[head, j, 32 * head + 16 + wide[j]] = 1.0
                bwd[head, j, 32 * head + high[j]] = 1.0
                bwd[head, j, 32 * head + 16 + 13 - wide[j]] = 1.0
            else:
                fwd[head, j, 32 * head + 14] = -1e30
    fwd = np.concatenate([fwd, fwd], axis=-1)
    return jnp.asarray(fwd, jnp.bfloat16), jnp.asarray(bwd, jnp.bfloat16)


def lane_iota(shape):
    return lax.broadcasted_iota(jnp.int32, shape, 1)


def head_mask(values, head, low):
    lane = lane_iota(values.shape) + low
    inside = (lane >= HEAD_DIM * head) & (lane < HEAD_DIM * head + HEAD_DIM)
    return jnp.where(inside, values, jnp.zeros_like(values))


def shift_lanes(values, amount):
    wide = values.astype(jnp.float32)
    return pltpu.roll(wide, amount % wide.shape[1], 1)


def load_group(qkv_ref, part, first):
    rows = qkv_ref.shape[1]
    q = qkv_ref[part, first:first + 16, :, 0:384].reshape(16 * SIDE, 384)
    k = qkv_ref[part, :, :, 256:640].reshape(rows * SIDE, 384)
    k = shift_lanes(k, -64).astype(jnp.bfloat16)
    v = qkv_ref[part, :, :, 640:960].reshape(rows * SIDE, 320)
    return q, k, v


def bias_rows(q, tables, first):
    along = dot(q, tables, NT) * (HEAD_DIM ** 0.5)
    high, wide = along[:, :128], along[:, 128:]
    pieces = []
    lane = lane_iota((SIDE, 128)) % 32
    for row in range(16):
        ih = (first + row) % WIN
        rows = slice(row * SIDE, (row + 1) * SIDE)
        up = pltpu.roll(high[rows], (ih - 13) % 128, 1)
        across = pltpu.roll(wide[rows], 3, 1, stride=1, stride_axis=0)
        both = jnp.where(lane < 16, up, across)
        pieces.append(jnp.where(lane == 14, 1.0, both))
    both = jnp.concatenate(pieces)
    upper = both.astype(jnp.bfloat16)
    lower = (both - upper.astype(jnp.float32)).astype(jnp.bfloat16)
    return jnp.concatenate([upper, lower], axis=1)


def softmax_rows(q, k, bias, select, head, split):
    low, high = SLABS[head]
    left = jnp.concatenate([q[:, low:high], bias], axis=1)
    sides = []
    for side, rows in ((0, slice(0, split)), (1, slice(split, 16 * SIDE))):
        keys = head_mask(k[side * KEYS:(side + 1) * KEYS, low:high], head, low)
        sides.append(dot(left[rows], jnp.concatenate([keys, select], axis=1), NT))
    scores = jnp.concatenate(sides)
    top = jnp.max(scores, axis=1, keepdims=True)
    raised = jnp.exp2((scores - top) * (SCALE * LOG2E))
    total = jnp.sum(raised, axis=1, keepdims=True)
    return raised * (1.0 / total)


def forward_body(first, qkv_ref, table_ref, select_ref, out_ref, acc):
    split = (WIN - first) * SIDE
    for part in range(2):
        q, k, v = load_group(qkv_ref, part, first)
        bias = bias_rows(q, table_ref[...], first)
        for head in range(GROUP):
            low, high = SLABS[head]
            high = min(high, 320)
            probs = softmax_rows(q, k, bias, select_ref[head], head, split).astype(jnp.bfloat16)
            sides = []
            for side, rows in ((0, slice(0, split)), (1, slice(split, 16 * SIDE))):
                values = head_mask(v[side * KEYS:(side + 1) * KEYS, low:high], head, low)
                sides.append(dot(probs[rows], values, NN))
            piece = jnp.concatenate(sides)
            if head == 0:
                acc[part, :, 0:128] = piece
                acc[part, :, 128:384] = jnp.zeros((16 * SIDE, 256), jnp.float32)
            else:
                acc[part, :, low:high] += piece
    second = pltpu.roll(acc[1], 64, 1)
    middle = acc[0, :, 256:384] + second[:, 0:128]
    whole = jnp.concatenate([acc[0, :, 0:256], middle, second[:, 128:384]], axis=1)
    out_ref[...] = whole.astype(jnp.bfloat16).reshape(16, SIDE, 640)


def by_shard(shard_ref, body):
    for shard in range(4):
        @pl.when(shard_ref[0] == shard)
        def _():
            body(2 * shard)


def forward_kernel(shard_ref, qkv_ref, table_ref, select_ref, out_ref, acc):
    by_shard(shard_ref, lambda first: forward_body(first, qkv_ref, table_ref, select_ref, out_ref, acc))


def window_attend(shard, qkv, tables, select):
    spec = pltpu.PrefetchScalarGridSpec(
        num_scalar_prefetch=1,
        grid=(5, 2),
        in_specs=[
            pl.BlockSpec((2, 28, SIDE, 960), lambda w, p, s: (p, 0, w, 0)),
            pl.BlockSpec((256, 384), lambda w, p, s: (0, 0)),
            pl.BlockSpec((GROUP, KEYS, 256), lambda w, p, s: (0, 0, 0)),
        ],
        out_specs=pl.BlockSpec((16, SIDE, 640), lambda w, p, s: (0, w, p)),
        scratch_shapes=[pltpu.VMEM((2, 16 * SIDE, 384), jnp.float32)],
    )
    return pl.pallas_call(
        forward_kernel,
        grid_spec=spec,
        out_shape=jax.ShapeDtypeStruct((16, 5 * SIDE, 1280), jnp.bfloat16),
        compiler_params=pltpu.CompilerParams(vmem_limit_bytes=48 << 20),
        cost_estimate=pl.CostEstimate(flops=1_000_000, bytes_accessed=1_000_000, transcendentals=0),
        name="attend",
    )(shard, qkv, tables, select)


def backward_body(first, qkv_ref, grad_ref, table_ref, back_ref, select_ref, spread_ref, out_ref, sums_ref, dq, dk, dv):
    split = (WIN - first) * SIDE
    queries = 16 * SIDE
    ranges = ((0, slice(0, split)), (1, slice(split, queries)))
    zero = jnp.zeros((queries, 128), jnp.float32)
    lane = lane_iota((SIDE, 128)) % 32
    for part in range(2):
        q, k, v = load_group(qkv_ref, part, first)
        if part == 0:
            go = grad_ref[:, :, 0:384].reshape(queries, 384)
        else:
            go = shift_lanes(grad_ref[:, :, 256:640].reshape(queries, 384), -64).astype(jnp.bfloat16)
        bias = bias_rows(q, table_ref[...], first)
        dq[...] = jnp.zeros_like(dq)
        dk[...] = jnp.zeros_like(dk)
        dv[...] = jnp.zeros_like(dv)
        marks = zero
        for head in range(GROUP):
            low, high = SLABS[head]
            vhigh = min(high, 320)
            probs = softmax_rows(q, k, bias, select_ref[head], head, split)
            probs_low = probs.astype(jnp.bfloat16)
            sides = []
            for side, rows in ranges:
                values = head_mask(v[side * KEYS:(side + 1) * KEYS, low:vhigh], head, low)
                sides.append(dot(go[rows, low:vhigh], values, NT))
            probs_grad = jnp.concatenate(sides)
            weighted = probs * probs_grad
            scores_grad = weighted - probs * jnp.sum(weighted, axis=1, keepdims=True)
            scores_low = scores_grad.astype(jnp.bfloat16)
            go_head = head_mask(go[:, low:high], head, low)
            q_head = head_mask(q[:, low:high], head, low)
            for side, rows in ranges:
                span = slice(side * KEYS, (side + 1) * KEYS)
                dv[span, low:high] += dot(probs_low[rows], go_head[rows], TN)
                dk[span, low:high] += dot(scores_low[rows], q_head[rows], TN)
                keys = head_mask(k[span, low:high], head, low)
                dq[rows, low:high] += dot(scores_low[rows], keys, NN)
            marks = marks + dot(scores_low, spread_ref[head], NN)
        highs, wides = [], []
        for row in range(16):
            ih = (first + row) % WIN
            piece = marks[row * SIDE:(row + 1) * SIDE]
            highs.append(pltpu.roll(jnp.where(lane < 14, piece, 0.0), (13 - ih) % 128, 1))
            across = jnp.where((lane >= 16) & (lane < 30), piece, 0.0)
            wides.append(pltpu.roll(across, 112, 1, stride=1, stride_axis=0))
        ranks = jnp.concatenate([jnp.concatenate(highs), jnp.concatenate(wides)], axis=1).astype(jnp.bfloat16)
        dq_full = dq[...] * SCALE + dot(ranks, back_ref[...], NN)
        sums_ref[...] += dot(ranks, q, TN)
        before, after = first * SIDE, (28 - 16 - first) * SIDE
        pieces = [dq_full]
        if before:
            pieces = [jnp.zeros((before, 384), jnp.float32)] + pieces
        if after:
            pieces = pieces + [jnp.zeros((after, 384), jnp.float32)]
        dq_all = jnp.concatenate(pieces) if len(pieces) > 1 else dq_full
        dk_all = pltpu.roll(dk[...] * SCALE, 64, 1)
        joint = lane_iota((28 * SIDE, 128))
        middle = jnp.where(joint < 64, dq_all[:, 256:384], dk_all[:, 0:128])
        left = jnp.concatenate([dq_all[:, 0:256], middle, dk_all[:, 128:384]], axis=1)
        out_ref[part, :, :, 0:640] = left.astype(jnp.bfloat16).reshape(28, SIDE, 640)
        out_ref[part, :, :, 640:960] = dv[:, 0:320].astype(jnp.bfloat16).reshape(28, SIDE, 320)


def backward_kernel(shard_ref, qkv_ref, grad_ref, table_ref, back_ref, select_ref, spread_ref, out_ref, sums_ref, dq, dk, dv):
    @pl.when(pl.program_id(0) == 0)
    def _():
        sums_ref[...] = jnp.zeros_like(sums_ref)

    by_shard(shard_ref, lambda first: backward_body(first, qkv_ref, grad_ref, table_ref, back_ref, select_ref, spread_ref, out_ref, sums_ref, dq, dk, dv))


def window_attend_back(pair, shard, qkv, grad, tables, back, select, spread):
    spec = pltpu.PrefetchScalarGridSpec(
        num_scalar_prefetch=1,
        grid=(5,),
        in_specs=[
            pl.BlockSpec((2, 28, SIDE, 960), lambda w, s: (pair, 0, w, 0)),
            pl.BlockSpec((16, SIDE, 640), lambda w, s: (0, w, pair)),
            pl.BlockSpec((256, 384), lambda w, s: (0, 0)),
            pl.BlockSpec((256, 384), lambda w, s: (0, 0)),
            pl.BlockSpec((GROUP, KEYS, 256), lambda w, s: (0, 0, 0)),
            pl.BlockSpec((GROUP, KEYS, 128), lambda w, s: (0, 0, 0)),
        ],
        out_specs=[
            pl.BlockSpec((2, 28, SIDE, 960), lambda w, s: (0, 0, w, 0)),
            pl.BlockSpec((256, 384), lambda w, s: (0, 0)),
        ],
        scratch_shapes=[
            pltpu.VMEM((16 * SIDE, 384), jnp.float32),
            pltpu.VMEM((2 * KEYS, 384), jnp.float32),
            pltpu.VMEM((2 * KEYS, 384), jnp.float32),
        ],
    )
    return pl.pallas_call(
        backward_kernel,
        grid_spec=spec,
        out_shape=[
            jax.ShapeDtypeStruct((2, 28, 5 * SIDE, 960), jnp.bfloat16),
            jax.ShapeDtypeStruct((256, 384), jnp.float32),
        ],
        compiler_params=pltpu.CompilerParams(vmem_limit_bytes=48 << 20),
        cost_estimate=pl.CostEstimate(flops=1_000_000, bytes_accessed=1_000_000, transcendentals=0),
        name="attend_back",
    )(shard, qkv, grad, tables, back, select, spread)


def project_kernel(shard_ref, x_ref, w_ref, bias_ref, out_ref):
    weights = w_ref[0][:, :960]
    for start in range(0, x_ref.shape[0], 448):
        rows = slice(start, start + 448)
        out_ref[0, rows, :] = (dot(x_ref[rows, :], weights, NN) + bias_ref[0]).astype(jnp.bfloat16)


def project(shard, x, weights, bias):
    tokens = x.shape[0]
    spec = pltpu.PrefetchScalarGridSpec(
        num_scalar_prefetch=1,
        grid=(4,),
        in_specs=[
            pl.BlockSpec((tokens, x.shape[1]), lambda p, s: (0, 0)),
            pl.BlockSpec((1,) + weights.shape[1:], lambda p, s: (p ^ s[0], 0, 0)),
            pl.BlockSpec((1, 1, 960), lambda p, s: (p ^ s[0], 0, 0)),
        ],
        out_specs=pl.BlockSpec((1, tokens, 960), lambda p, s: (p, 0, 0)),
    )
    return pl.pallas_call(
        project_kernel,
        grid_spec=spec,
        out_shape=jax.ShapeDtypeStruct((4, tokens, 960), jnp.bfloat16),
        compiler_params=pltpu.CompilerParams(vmem_limit_bytes=48 << 20),
        cost_estimate=pl.CostEstimate(flops=1_000_000, bytes_accessed=1_000_000, transcendentals=0),
        name="project",
    )(shard, x, weights, bias)


ROWS = 16
FRAME = 28
EARLY, LATE = 6, 12
EPSILON = 1e-06


def swap(values, shifts):
    return lax.ppermute(values, "tensor", shifts)


def own(values, index, axis=0):
    return lax.dynamic_index_in_dim(values, index, axis, keepdims=False)


def gather_small(values, shard):
    parts = [values]
    for step in (1, 2, 3):
        parts.append(swap(values, [(i, (i + step) % 4) for i in range(4)]))
    stack = jnp.stack(parts)
    return jnp.stack([own(stack, (shard - i) % 4) for i in range(4)])


CORES = [(0, 1), (1, 0), (2, 3), (3, 2)]
SIDES = [(0, 2), (2, 0), (1, 3), (3, 1)]


def add_low(left, right):
    return (left.astype(jnp.float32) + right.astype(jnp.float32)).astype(jnp.bfloat16)


def scatter_dp(quarter):
    return lax.psum_scatter(quarter, "dp", scatter_dimension=0, tiled=True)


def after(first, *values):
    return lax.optimization_barrier((first,) + values)[1:]


def sum_everywhere(values):
    values = values + swap(values, CORES)
    values = values + swap(values, SIDES)
    count = lax.axis_size("dp")
    step = 1
    while step < count:
        values = values + lax.ppermute(values, "dp", [(i, i ^ step) for i in range(count)])
        step *= 2
    return values


def statistics(values):
    average = jnp.mean(values, axis=-1, keepdims=True)
    centred = values - average
    rstd = lax.rsqrt(jnp.mean(centred * centred, axis=-1, keepdims=True) + EPSILON)
    return centred * rstd, rstd


def norm_back(grad, gain, hat, rstd):
    scaled = grad * gain
    mean_one = jnp.mean(scaled, axis=-1, keepdims=True)
    mean_two = jnp.mean(scaled * hat, axis=-1, keepdims=True)
    return rstd * (scaled - mean_one - hat * mean_two)


def column_selector():
    column = np.arange(GRID)
    place = SIDE * (column // WIN) + column % WIN
    select = np.zeros((NWIN * SIDE, GRID), np.float32)
    select[place, column] = 1.0
    return jnp.asarray(select, jnp.bfloat16)


def fast_shards(
    inputs,
    cotangent,
    teacher,
    qkv_weight,
    proj_weight,
    up_weight,
    down_weight,
    qv_bias,
    up_bias,
    norm_gains,
    norm_shifts,
    out_biases,
    rel_tables,
):
    f32, bf16 = jnp.float32, jnp.bfloat16
    shard = lax.axis_index("tensor")
    both = ("tensor", "dp")
    tokens = ROWS * GRID
    inner = qkv_weight.shape[1]
    joint = jnp.concatenate([qkv_weight.transpose(1, 0, 2).reshape(inner, 960), proj_weight.T], axis=1)
    joint_all = lax.all_gather(joint, both, axis=0, tiled=True)
    joint_all = joint_all.reshape(4, D, 1280)
    biases = gather_small(jnp.concatenate([qv_bias.reshape(-1), up_bias]), shard)
    qkv_bias = jnp.concatenate(
        [biases[:, :320], jnp.zeros((4, 320), bf16), biases[:, 320:640]], axis=1
    ).astype(f32)
    up_bias_all = biases[:, 640:].astype(f32)

    gains = norm_gains.astype(f32)
    shifts = norm_shifts.astype(f32)
    image = inputs[0]
    above = swap(image[ROWS - EARLY:], [(i, i + 1) for i in range(3)])
    below = swap(image[:LATE], [(i + 1, i) for i in range(3)])
    framed = lax.dynamic_slice_in_dim(
        jnp.concatenate([above, image, below]), EARLY - 2 * shard, FRAME, 0
    )
    frame_hat, _ = statistics(framed.astype(f32))
    inside = (WIN * shard + jnp.arange(FRAME) < GRID)[:, None, None]
    normed = jnp.where(inside, frame_hat * gains[0] + shifts[0], 0.0).astype(bf16)
    select = column_selector()
    windows = jnp.einsum("pc,rcd->rpd", select, normed, preferred_element_type=f32).astype(bf16)
    flat = windows.reshape(FRAME * NWIN * SIDE, D)
    where = shard[None].astype(jnp.int32)
    qkv = project(where, flat, joint_all, qkv_bias[:, None, :])
    qkv = qkv.reshape(4, FRAME, NWIN * SIDE, 960)
    tables, back_tables = bias_tables(rel_tables)
    select_keys, spread_keys = selectors()
    (up_shard,) = after((joint_all, flat), up_weight)
    up_all = lax.all_gather(up_shard, both, axis=0, tiled=True).reshape(4, D, 1280)
    joint_own = [own(joint_all, shard ^ p) for p in range(4)]
    proj_full = jnp.concatenate([part[:, 960:] for part in joint_own], axis=1)
    attended = window_attend(where, qkv, tables, select_keys)
    attended = jnp.einsum("pc,rpd->rcd", select, attended, preferred_element_type=f32)
    attended = attended.astype(bf16).reshape(tokens, D)

    (down_shard,) = after(attended, down_weight.T)
    down_all = lax.all_gather(down_shard, both, axis=0, tiled=True).reshape(4, D, 1280)
    source = image.astype(f32).reshape(tokens, D)
    branch = jnp.einsum("nk,ck->nc", attended, proj_full, preferred_element_type=f32)
    middle = source + branch + out_biases[0].astype(f32)
    second_hat, second_rstd = statistics(middle)
    normed_two = (second_hat * gains[1] + shifts[1]).astype(bf16)
    hidden = jnp.einsum("nd,tdm->tnm", normed_two, up_all, preferred_element_type=f32)
    hidden = hidden + up_bias_all[:, None, :]
    cdf = 0.5 + 0.5 * lax.erf(hidden * (0.5 ** 0.5))
    active = (hidden * cdf).astype(bf16)
    slope = (cdf + hidden * (jnp.exp(-0.5 * hidden * hidden) * (0.5 / np.pi) ** 0.5)).astype(bf16)
    result = jnp.einsum("tnm,tcm->nc", active, down_all, preferred_element_type=f32)
    result = middle + result + out_biases[1].astype(f32)
    mismatch = result - teacher[0].astype(f32).reshape(tokens, D)
    loss_total = jnp.sum(mismatch * mismatch)
    output = result.astype(bf16)

    result_grad = cotangent[0].astype(f32).reshape(tokens, D) + mismatch
    result_low = result_grad.astype(bf16)
    def down_block(p):
        return jnp.einsum("nc,nm->cm", result_low, own(active, shard ^ p), preferred_element_type=f32)

    sends = [down_block(3).astype(bf16), down_block(1).astype(bf16)]
    down_three, down_one = swap(sends[0], CORES), swap(sends[1], CORES)
    (result_next,) = after(tuple(sends), result_low)
    active_grad = jnp.einsum("nc,tcm->tnm", result_next, down_all, preferred_element_type=f32)
    hidden_grad = active_grad * slope.astype(f32)
    up_bias_acc = jnp.sum(hidden_grad, axis=1)
    hidden_low = hidden_grad.astype(bf16)
    down_far = (down_block(2) + down_three.astype(f32)).astype(bf16)
    down_near = (down_block(0) + down_one.astype(f32)).astype(bf16)
    down_side = swap(down_far, SIDES)
    hidden_low, normed_two = after((down_far, down_near), hidden_low, normed_two)

    def up_block(p):
        return jnp.einsum("nd,nm->dm", normed_two, own(hidden_low, shard ^ p), preferred_element_type=f32)

    sends = [up_block(3).astype(bf16), up_block(1).astype(bf16)]
    up_three, up_one = swap(sends[0], CORES), swap(sends[1], CORES)
    (hidden_next,) = after(tuple(sends), hidden_low)
    second_grad = jnp.einsum("tnm,tdm->nd", hidden_next, up_all, preferred_element_type=f32)
    middle_grad = result_grad + norm_back(second_grad, gains[1], second_hat, second_rstd)
    second_gain = jnp.sum(second_grad * second_hat, axis=0)
    second_shift = jnp.sum(second_grad, axis=0)
    middle_low = middle_grad.astype(bf16)
    attended_grad = jnp.einsum("nc,ck->nk", middle_low, proj_full, preferred_element_type=f32)
    attended_grad = attended_grad.astype(bf16).reshape(ROWS, GRID, D)
    attended_grad = jnp.einsum("pc,rcd->rpd", select, attended_grad, preferred_element_type=f32)
    attended_grad = attended_grad.astype(bf16)
    up_far = (up_block(2) + up_three.astype(f32)).astype(bf16)
    up_near = (up_block(0) + up_one.astype(f32)).astype(bf16)
    up_side = swap(up_far, SIDES)

    def proj_block(p):
        part = attended[:, 320 * p:320 * p + 320]
        return jnp.einsum("nc,nk->ck", middle_low, part, preferred_element_type=f32)

    proj_three = swap(proj_block(3).astype(bf16), CORES)
    proj_one = swap(proj_block(1).astype(bf16), CORES)
    down_quarter = add_low(down_near, down_side)
    down_grad = scatter_dp(down_quarter)
    (grad_far,) = after((up_far, up_near, down_quarter), attended_grad)
    far_back, far_sums = window_attend_back(
        1, where, qkv, grad_far, tables, back_tables, select_keys, spread_keys
    )
    proj_far = (proj_block(2) + proj_three.astype(f32)).astype(bf16)
    proj_near = (proj_block(0) + proj_one.astype(f32)).astype(bf16)
    far_back = far_back.reshape(2, FRAME * NWIN * SIDE, 960)

    def qkv_block(back):
        return jnp.einsum("nd,nc->dc", flat, back, preferred_element_type=f32)

    qkv_three = swap(qkv_block(far_back[1]).astype(bf16), CORES)
    qkv_far = (qkv_block(far_back[0]) + qkv_three.astype(f32)).astype(bf16)
    far_side = swap(jnp.concatenate([qkv_far, proj_far], axis=1), SIDES)
    (grad_near,) = after((qkv_far, proj_far), attended_grad)
    near_back, near_sums = window_attend_back(
        0, where, qkv, grad_near, tables, back_tables, select_keys, spread_keys
    )
    near_back = near_back.reshape(2, FRAME * NWIN * SIDE, 960)
    up_quarter = add_low(up_near, up_side)
    up_grad = scatter_dp(up_quarter)
    near_back, flat = after(up_quarter, near_back, flat)
    qkv_one = swap(qkv_block(near_back[1]).astype(bf16), CORES)
    qkv_near = qkv_block(near_back[0]) + qkv_one.astype(f32)
    near = jnp.concatenate([qkv_near.astype(bf16), proj_near], axis=1)
    joint_quarter = add_low(near, far_side)
    joint_grad = scatter_dp(joint_quarter)
    near_next, far_next = after(joint_quarter, near_back, far_back)
    table_sums = far_sums + near_sums
    bias_sums = jnp.concatenate([jnp.sum(near_next.astype(f32), axis=1), jnp.sum(far_next.astype(f32), axis=1)])
    qv_acc = jnp.stack([bias_sums[:, :320], bias_sums[:, 640:]], axis=1)
    qv_acc = jnp.stack([own(qv_acc, shard ^ t) for t in range(4)])
    table_sums = table_sums[:, :320].reshape(2, GROUP, 32, GROUP, HEAD_DIM)
    table_acc = jnp.einsum("phrhd->prd", table_sums)
    table_acc = jnp.stack([table_acc[0, :27][::-1], table_acc[1, :27]])
    weights = [part[:, :960] for part in joint_own]
    frame_grad = jnp.einsum("tnc,tdc->nd", far_next, jnp.stack(weights[2:]), preferred_element_type=f32)
    frame_grad = frame_grad + jnp.einsum("tnc,tdc->nd", near_next, jnp.stack(weights[:2]), preferred_element_type=f32)
    frame_grad = frame_grad.astype(bf16).reshape(FRAME, NWIN * SIDE, D)
    frame_grad = jnp.einsum("pc,rpd->rcd", select, frame_grad, preferred_element_type=f32).astype(bf16)
    spread = jnp.zeros((EARLY + ROWS + LATE, GRID, D), bf16)
    spread = lax.dynamic_update_slice_in_dim(spread, frame_grad, EARLY - 2 * shard, 0)
    from_next = swap(spread[:EARLY], [(i + 1, i) for i in range(3)])
    from_before = swap(spread[EARLY + ROWS:], [(i, i + 1) for i in range(3)])
    first_grad = spread[EARLY:EARLY + ROWS].astype(f32)
    first_grad = first_grad + jnp.pad(from_next.astype(f32), ((ROWS - EARLY, 0), (0, 0), (0, 0)))
    first_grad = first_grad + jnp.pad(from_before.astype(f32), ((0, ROWS - LATE), (0, 0), (0, 0)))
    first_grad = first_grad.reshape(tokens, D)
    first_hat, first_rstd = statistics(source)
    first_gain = jnp.sum(first_grad * first_hat, axis=0)
    first_shift = jnp.sum(first_grad, axis=0)
    input_grad = middle_grad + norm_back(first_grad, gains[0], first_hat, first_rstd)

    small = [
        qv_acc, up_bias_acc, first_gain, second_gain, first_shift, second_shift,
        jnp.sum(middle_grad, axis=0), jnp.sum(result_grad, axis=0), table_acc, loss_total,
    ]
    sums = sum_everywhere(jnp.concatenate([part.reshape(-1) for part in small]))
    parts = []
    place = 0
    for part in small:
        parts.append(sums[place:place + part.size].reshape(part.shape))
        place += part.size
    qv_sum, up_sum, gain_one, gain_two, shift_one, shift_two, bias_one, bias_two, table_grad, loss_sum = parts
    loss = loss_sum / (tokens * D * lax.axis_size("dp") * lax.axis_size("tensor"))
    return (
        output.reshape(1, ROWS, GRID, D),
        input_grad.reshape(1, ROWS, GRID, D),
        loss,
        joint_grad[:, :960].reshape(inner, 3, 320).transpose(1, 0, 2).astype(f32),
        joint_grad[:, 960:].T.astype(f32),
        up_grad.astype(f32),
        down_grad.T.astype(f32),
        own(qv_sum, shard),
        own(up_sum, shard),
        jnp.stack([gain_one, gain_two]),
        jnp.stack([shift_one, shift_two]),
        jnp.stack([bias_one, bias_two]),
        table_grad,
    )


def solution(mesh):
    in_specs = (
        P("dp", "tensor", None, None),
        P("dp", "tensor", None, None),
        P("dp", "tensor", None, None),
        P(None, "dp", "tensor"),
        P("tensor", "dp"),
        P("dp", "tensor"),
        P("tensor", "dp"),
        P(None, "tensor"),
        P("tensor"),
        P(),
        P(),
        P(),
        P(),
    )
    out_specs = (
        P("dp", "tensor", None, None),
        P("dp", "tensor", None, None),
        P(),
        P(None, "dp", "tensor"),
        P("tensor", "dp"),
        P("dp", "tensor"),
        P("tensor", "dp"),
        P(None, "tensor"),
        P("tensor"),
        P(),
        P(),
        P(),
        P(),
    )
    fits = mesh.shape["tensor"] == 4 and GRID // mesh.shape["tensor"] == 16
    shards = fast_shards if fits else general_shards
    return jax.shard_map(shards, mesh=mesh, in_specs=in_specs, out_specs=out_specs, check_vma=False)
```

```python
from functools import partial

import jax
import jax.numpy as jnp
import numpy as np
from jax import lax
from jax.experimental import pallas as pl
from jax.experimental.pallas import tpu as pltpu
from jax.sharding import PartitionSpec as P

D = 1280
HEAD_DIM = 80
GRID = 64
WIN = 14
PGRID = 70
NWIN = 5


highest = lax.Precision.HIGHEST


def layer_norm(values, gain_vector, shift_vector):
    average = jnp.mean(values, axis=-1, keepdims=True)
    centred = values - average
    variance = jnp.mean(centred * centred, axis=-1, keepdims=True)
    return centred * lax.rsqrt(variance + 1e-06) * gain_vector + shift_vector


def exact_gelu(values):
    return jax.nn.gelu(values, approximate=False)


def offset_tables(window):
    position = jnp.arange(window * window)
    across = jnp.arange(window)
    ranks = jnp.arange(2 * window - 1)
    high_sel = (
        position[:, None, None] // window - across[None, :, None] + window - 1
        == ranks[None, None, :]
    ).astype(jnp.float32)
    wide_sel = (
        position[:, None, None] % window - across[None, :, None] + window - 1
        == ranks[None, None, :]
    ).astype(jnp.float32)
    return (high_sel, wide_sel)


def to_windows(grid_values):
    extra = PGRID - GRID
    padded = jnp.pad(grid_values, ((0, extra), (0, extra), (0, 0)))
    channels = grid_values.shape[-1]
    shaped = padded.reshape(NWIN, WIN, NWIN, WIN, channels).transpose(0, 2, 1, 3, 4)
    return shaped.reshape(NWIN, NWIN, WIN * WIN, channels)


def from_windows(windowed):
    channels = windowed.shape[-1]
    shaped = windowed.reshape(NWIN, NWIN, WIN, WIN, channels).transpose(0, 2, 1, 3, 4)
    return shaped.reshape(PGRID, PGRID, channels)[:GRID, :GRID]


def score_block(queries, key_rows, tables, selectors):
    table_high, table_wide = tables
    high_sel, wide_sel = selectors
    raw = jnp.einsum(
        "wqhc,wkhc->whqk", queries, key_rows, preferred_element_type=jnp.float32
    ) * HEAD_DIM ** (-0.5)
    along_high = jnp.einsum(
        "wqhc,rc->wqhr", queries, table_high, preferred_element_type=jnp.float32
    )
    along_wide = jnp.einsum(
        "wqhc,rc->wqhr", queries, table_wide, preferred_element_type=jnp.float32
    )
    bias_high = jnp.einsum("wqhr,qkr->whqk", along_high, high_sel, precision=highest)
    bias_wide = jnp.einsum("wqhr,qkr->whqk", along_wide, wide_sel, precision=highest)
    shaped = (
        raw.reshape(raw.shape[:3] + (WIN, WIN)) + bias_high[..., :, None] + bias_wide[..., None, :]
    )
    return shaped.reshape(raw.shape)


def attend_row(block_parts, tables, selectors):
    queries, key_rows, value_rows = block_parts
    scores = score_block(queries, key_rows, tables, selectors)
    row_max = jnp.max(scores, axis=-1, keepdims=True)
    shifted = jnp.exp(scores - row_max)
    row_total = jnp.sum(shifted, axis=-1, keepdims=True)
    probs_low = (shifted / row_total).astype(jnp.bfloat16)
    attended = jnp.einsum(
        "whqk,wkhc->wqhc", probs_low, value_rows, preferred_element_type=jnp.float32
    )
    return (attended.astype(jnp.bfloat16), (row_max + jnp.log(row_total))[..., 0])


def attend_back(block_parts, tables, selectors):
    queries, key_rows, value_rows, attended_grad, log_total = block_parts
    high_sel, wide_sel = selectors
    scores = score_block(queries, key_rows, tables, selectors)
    probs = jnp.exp(scores - log_total[..., None])
    probs_grad = jnp.einsum(
        "wqhc,wkhc->whqk", attended_grad, value_rows, preferred_element_type=jnp.float32
    )
    value_grad = jnp.einsum(
        "whqk,wqhc->wkhc",
        probs.astype(jnp.bfloat16),
        attended_grad,
        preferred_element_type=jnp.float32,
    )
    scores_grad = probs * (probs_grad - jnp.sum(probs * probs_grad, axis=-1, keepdims=True))
    scores_low = scores_grad.astype(jnp.bfloat16)
    query_grad = jnp.einsum(
        "whqk,wkhc->wqhc", scores_low, key_rows, preferred_element_type=jnp.float32
    ) * HEAD_DIM ** (-0.5)
    key_grad = jnp.einsum(
        "whqk,wqhc->wkhc", scores_low, queries, preferred_element_type=jnp.float32
    ) * HEAD_DIM ** (-0.5)
    shaped = scores_grad.reshape(scores_grad.shape[:3] + (WIN, WIN))
    rank_high = jnp.einsum("whqa,qar->wqhr", jnp.sum(shaped, axis=-1), high_sel, precision=highest)
    rank_wide = jnp.einsum("whqb,qbr->wqhr", jnp.sum(shaped, axis=-2), wide_sel, precision=highest)
    table_high = tables[0].astype(jnp.float32)
    table_wide = tables[1].astype(jnp.float32)
    query_grad = query_grad + jnp.einsum("wqhr,rc->wqhc", rank_high, table_high, precision=highest)
    query_grad = query_grad + jnp.einsum("wqhr,rc->wqhc", rank_wide, table_wide, precision=highest)
    query_wide = queries.astype(jnp.float32)
    table_grad = jnp.stack(
        [
            jnp.einsum("wqhr,wqhc->rc", rank_high, query_wide, precision=highest),
            jnp.einsum("wqhr,wqhc->rc", rank_wide, query_wide, precision=highest),
        ]
    )
    return (query_grad, key_grad, value_grad, table_grad)


def general_shards(
    inputs,
    cotangent,
    teacher,
    qkv_weight,
    proj_weight,
    up_weight,
    down_weight,
    qv_bias,
    up_bias,
    norm_gains,
    norm_shifts,
    out_biases,
    rel_tables,
):
    qkv_full, proj_full, up_full, down_full = (
        lax.all_gather(qkv_weight, "dp", axis=1, tiled=True),
        lax.all_gather(proj_weight, "dp", axis=1, tiled=True),
        lax.all_gather(up_weight, "dp", axis=0, tiled=True),
        lax.all_gather(down_weight, "dp", axis=1, tiled=True),
    )
    up_matrix, down_matrix, up_bias_all = (up_full, down_full, up_bias)
    images, row_count = (inputs.shape[0], inputs.shape[1])
    local_width = qkv_full.shape[2]
    head_count = local_width // HEAD_DIM
    head_shape = (NWIN, NWIN, WIN * WIN, head_count, HEAD_DIM)
    selectors = offset_tables(WIN)
    tables = (rel_tables[0], rel_tables[1])
    gains_wide = norm_gains.astype(jnp.float32)
    shifts_wide = norm_shifts.astype(jnp.float32)
    source = inputs[0].astype(jnp.float32)
    normed = layer_norm(source, gains_wide[0], shifts_wide[0]).astype(jnp.bfloat16)
    gathered = lax.all_gather(normed, "tensor", axis=0, tiled=True)
    windows = to_windows(gathered)
    projected = jnp.einsum("abpd,sdc->sabpc", windows, qkv_full, preferred_element_type=jnp.float32)
    queries = (projected[0] + qv_bias[0]).astype(jnp.bfloat16).reshape(head_shape)
    key_rows = projected[1].astype(jnp.bfloat16).reshape(head_shape)
    value_rows = (projected[2] + qv_bias[1]).astype(jnp.bfloat16).reshape(head_shape)
    attended, log_totals = lax.map(
        partial(attend_row, tables=tables, selectors=selectors), (queries, key_rows, value_rows)
    )
    grid_out = from_windows(attended.reshape(NWIN, NWIN, WIN * WIN, local_width))
    row_piece = grid_out
    attn_branch = lax.psum_scatter(
        jnp.einsum("xyc,cd->xyd", row_piece, proj_full, preferred_element_type=jnp.float32).astype(
            jnp.bfloat16
        ),
        "tensor",
        scatter_dimension=0,
        tiled=True,
    ).astype(jnp.float32)
    middle = source + attn_branch + out_biases[0].astype(jnp.float32)
    normed_two = layer_norm(middle, gains_wide[1], shifts_wide[1]).astype(jnp.bfloat16)
    mlp_input = lax.all_gather(normed_two, "tensor", axis=0, tiled=True)
    hidden = (
        jnp.einsum("xyd,dm->xym", mlp_input, up_matrix, preferred_element_type=jnp.float32)
        + up_bias_all
    )
    active = exact_gelu(hidden).astype(jnp.bfloat16)
    row_piece = active
    mlp_branch = lax.psum_scatter(
        jnp.einsum(
            "xym,md->xyd", row_piece, down_matrix, preferred_element_type=jnp.float32
        ).astype(jnp.bfloat16),
        "tensor",
        scatter_dimension=0,
        tiled=True,
    ).astype(jnp.float32)
    result = middle + mlp_branch + out_biases[1].astype(jnp.float32)
    mismatch = result - teacher[0].astype(jnp.float32)
    loss_total = jnp.sum(mismatch * mismatch)
    outputs = [result.astype(jnp.bfloat16)]
    result_grad = cotangent[0].astype(jnp.float32) + mismatch
    result_low = result_grad.astype(jnp.bfloat16)
    grad_rows = lax.all_gather(result_low, "tensor", axis=0, tiled=True)
    down_acc = jnp.einsum("xym,xyd->md", active, grad_rows, preferred_element_type=jnp.float32)
    active_grad = jnp.einsum(
        "xyd,md->xym", grad_rows, down_matrix, preferred_element_type=jnp.float32
    )
    gelu_value, gelu_back = jax.vjp(exact_gelu, hidden)
    hidden_grad = gelu_back(active_grad)[0]
    up_bias_acc = jnp.sum(hidden_grad, axis=(0, 1))
    hidden_low = hidden_grad.astype(jnp.bfloat16)
    up_acc = jnp.einsum("xyd,xym->dm", mlp_input, hidden_low, preferred_element_type=jnp.float32)
    row_piece = hidden_low
    second_grad = lax.psum_scatter(
        jnp.einsum("xym,dm->xyd", row_piece, up_matrix, preferred_element_type=jnp.float32).astype(
            jnp.bfloat16
        ),
        "tensor",
        scatter_dimension=0,
        tiled=True,
    ).astype(jnp.float32)
    second_value, second_back = jax.vjp(layer_norm, middle, gains_wide[1], shifts_wide[1])
    middle_part, second_gain, second_shift = second_back(second_grad)
    middle_grad = result_grad + middle_part
    out_bias_acc = jnp.stack([jnp.sum(middle_grad, axis=(0, 1)), jnp.sum(result_grad, axis=(0, 1))])
    middle_low = middle_grad.astype(jnp.bfloat16)
    gathered_grad = lax.all_gather(middle_low, "tensor", axis=0, tiled=True)
    proj_acc = jnp.einsum(
        "xyc,xyd->cd", grid_out, gathered_grad, preferred_element_type=jnp.float32
    )
    attended_grad = jnp.einsum(
        "xyd,cd->xyc", gathered_grad, proj_full, preferred_element_type=jnp.float32
    ).astype(jnp.bfloat16)
    grad_windows = to_windows(attended_grad).reshape(head_shape)
    query_grad, key_grad, value_grad, table_parts = lax.map(
        partial(attend_back, tables=tables, selectors=selectors),
        (queries, key_rows, value_rows, grad_windows, log_totals),
    )
    table_acc = jnp.sum(table_parts, axis=0)
    query_flat = query_grad.reshape(NWIN, NWIN, WIN * WIN, local_width)
    key_flat = key_grad.reshape(NWIN, NWIN, WIN * WIN, local_width)
    value_flat = value_grad.reshape(NWIN, NWIN, WIN * WIN, local_width)
    qv_acc = jnp.stack([jnp.sum(query_flat, axis=(0, 1, 2)), jnp.sum(value_flat, axis=(0, 1, 2))])
    stacked = jnp.stack([query_flat, key_flat, value_flat]).astype(jnp.bfloat16)
    qkv_acc = jnp.einsum("abpd,sabpc->sdc", windows, stacked, preferred_element_type=jnp.float32)
    normed_back = jnp.einsum(
        "sabpc,sdc->abpd", stacked, qkv_full, preferred_element_type=jnp.float32
    )
    first_grad = lax.psum_scatter(
        from_windows(normed_back).astype(jnp.bfloat16), "tensor", scatter_dimension=0, tiled=True
    ).astype(jnp.float32)
    first_value, first_back = jax.vjp(layer_norm, source, gains_wide[0], shifts_wide[0])
    source_part, first_gain, first_shift = first_back(first_grad)
    gain_acc = jnp.stack([first_gain, second_gain])
    shift_acc = jnp.stack([first_shift, second_shift])
    input_grads = [middle_grad + source_part]
    qkv_grad, proj_grad, up_grad, down_grad = (
        lax.psum_scatter(
            qkv_acc.astype(jnp.bfloat16), "dp", scatter_dimension=1, tiled=True
        ).astype(jnp.float32),
        lax.psum_scatter(
            proj_acc.astype(jnp.bfloat16), "dp", scatter_dimension=1, tiled=True
        ).astype(jnp.float32),
        lax.psum_scatter(up_acc.astype(jnp.bfloat16), "dp", scatter_dimension=0, tiled=True).astype(
            jnp.float32
        ),
        lax.psum_scatter(
            down_acc.astype(jnp.bfloat16), "dp", scatter_dimension=1, tiled=True
        ).astype(jnp.float32),
    )
    qv_grad, up_bias_grad = lax.psum((qv_acc, up_bias_acc), "dp")
    gains_grad, shifts_grad, out_grad, table_grad, loss_sum = lax.psum(
        (gain_acc, shift_acc, out_bias_acc, table_acc, loss_total), ("dp", "tensor")
    )
    element_count = images * row_count * GRID * D * lax.axis_size("dp") * lax.axis_size("tensor")
    loss = loss_sum / element_count
    return (
        jnp.stack(outputs),
        jnp.stack(input_grads),
        loss,
        qkv_grad,
        proj_grad,
        up_grad,
        down_grad,
        qv_grad,
        up_bias_grad,
        gains_grad,
        shifts_grad,
        out_grad,
        table_grad,
    )


SIDE = 16
GROUP = 4
KEYS = WIN * SIDE
SLABS = ((0, 128), (0, 256), (128, 256), (128, 384))
SCALE = HEAD_DIM ** (-0.5)
LOG2E = 1.4426950408889634
NT = (((1,), (1,)), ((), ()))
TN = (((0,), (0,)), ((), ()))
NN = (((1,), (0,)), ((), ()))


def dot(a, b, dims):
    return lax.dot_general(a, b, dims, preferred_element_type=jnp.float32)


def bias_tables(rel_tables):
    tables = rel_tables.astype(jnp.bfloat16)

    def place(rows):
        padded = jnp.pad(rows, ((0, 5), (0, 0)))
        eye = jnp.eye(GROUP, dtype=jnp.bfloat16)
        spread = eye[:, None, :, None] * padded[None, :, None, :]
        return spread.reshape(GROUP * 32, GROUP * HEAD_DIM)

    forward = jnp.concatenate([place(tables[0][::-1]), place(tables[1][::-1])])
    backward = jnp.concatenate([place(tables[0][::-1]), place(tables[1])])
    lanes = ((0, 0), (0, 64))
    return jnp.pad(forward, lanes), jnp.pad(backward, lanes)


def selectors():
    key = np.arange(KEYS)
    high, wide = key // SIDE, key % SIDE
    fwd = np.zeros((GROUP, KEYS, 128), np.float32)
    bwd = np.zeros((GROUP, KEYS, 128), np.float32)
    real = wide < WIN
    for head in range(GROUP):
        for j in range(KEYS):
            if real[j]:
                fwd[head, j, 32 * head + high[j]] = 1.0
                fwd[head, j, 32 * head + 16 + wide[j]] = 1.0
                bwd[head, j, 32 * head + high[j]] = 1.0
                bwd[head, j, 32 * head + 16 + 13 - wide[j]] = 1.0
            else:
                fwd[head, j, 32 * head + 14] = -1e30
    fwd = np.concatenate([fwd, fwd], axis=-1)
    return jnp.asarray(fwd, jnp.bfloat16), jnp.asarray(bwd, jnp.bfloat16)


def lane_iota(shape):
    return lax.broadcasted_iota(jnp.int32, shape, 1)


def head_mask(values, head, low):
    lane = lane_iota((1, values.shape[1])) + low
    inside = (lane >= HEAD_DIM * head) & (lane < HEAD_DIM * head + HEAD_DIM)
    return values * inside.astype(jnp.float32).astype(jnp.bfloat16)


def shift_lanes(values, amount):
    wide = values.astype(jnp.float32)
    return pltpu.roll(wide, amount % wide.shape[1], 1)


def load_group(qkv_ref, part, first):
    rows = qkv_ref.shape[1]
    q = qkv_ref[part, pl.ds(first, 16), :, 0:384].reshape(16 * SIDE, 384)
    k = qkv_ref[part, :, :, 256:640].reshape(rows * SIDE, 384)
    k = shift_lanes(k, -64).astype(jnp.bfloat16)
    v = qkv_ref[part, :, :, 640:960].reshape(rows * SIDE, 320)
    return q, k, v


def by_side(values, first):
    row = lax.broadcasted_iota(jnp.int32, (16 * SIDE, 1), 0)
    upper = (row < (WIN - first) * SIDE).astype(jnp.float32)
    return values * upper.astype(jnp.bfloat16), values * (1.0 - upper).astype(jnp.bfloat16)


def bias_rows(q, tables, first):
    along = dot(q, tables, NT) * (HEAD_DIM ** 0.5)
    high, wide = along[:, :128], along[:, 128:]
    pieces = []
    lane = lane_iota((SIDE, 128)) % 32
    for row in range(16):
        ih = lax.rem(first + row, WIN)
        rows = slice(row * SIDE, (row + 1) * SIDE)
        up = pltpu.roll(high[rows], lax.rem(ih + 115, 128), 1)
        across = pltpu.roll(wide[rows], 3, 1, stride=1, stride_axis=0)
        both = jnp.where(lane < 16, up, across)
        pieces.append(jnp.where(lane == 14, 1.0, both))
    both = jnp.concatenate(pieces)
    upper = both.astype(jnp.bfloat16)
    lower = (both - upper.astype(jnp.float32)).astype(jnp.bfloat16)
    return jnp.concatenate([upper, lower], axis=1)


def beside(upper, lower):
    return jnp.concatenate([upper, lower], axis=1)


def softmax_rows(q_sides, keys, bias, select, head):
    low, high = SLABS[head]
    left = jnp.concatenate([q_sides[0][:, low:high], q_sides[1][:, low:high], bias], axis=1)
    right = jnp.concatenate([keys[:KEYS], keys[KEYS:], select], axis=1)
    scores = dot(left, right, NT)
    top = jnp.max(scores, axis=1, keepdims=True)
    raised = jnp.exp2((scores - top) * (SCALE * LOG2E))
    total = jnp.sum(raised, axis=1, keepdims=True)
    return raised * (1.0 / total)


def pick_side(both, first):
    width = both.shape[1] // 2
    row = lax.broadcasted_iota(jnp.int32, (16 * SIDE, 1), 0)
    return jnp.where(row < (WIN - first) * SIDE, both[:, :width], both[:, width:])


def pad_lanes(values, width):
    missing = width - values.shape[1]
    if missing == 0:
        return values
    return jnp.concatenate([values, jnp.zeros((values.shape[0], missing), values.dtype)], axis=1)


def forward_kernel(shard_ref, qkv_ref, table_ref, select_ref, out_ref, acc):
    first = 2 * shard_ref[0]
    for part in range(2):
        q, k, v = load_group(qkv_ref, part, first)
        q_sides = by_side(q, first)
        bias = bias_rows(q, table_ref[...], first)
        v = pad_lanes(v, 384)
        for head in range(GROUP):
            low, high = SLABS[head]
            keys = head_mask(k[:, low:high], head, low)
            probs = softmax_rows(q_sides, keys, bias, select_ref[head], head).astype(jnp.bfloat16)
            values = head_mask(v[:, low:high], head, low)
            piece = pick_side(dot(probs, beside(values[:KEYS], values[KEYS:]), NN), first)
            if head == 0:
                acc[part, :, 0:128] = piece
                acc[part, :, 128:384] = jnp.zeros((16 * SIDE, 256), jnp.float32)
            else:
                acc[part, :, low:high] += piece
    second = pltpu.roll(acc[1], 64, 1)
    middle = acc[0, :, 256:384] + second[:, 0:128]
    whole = jnp.concatenate([acc[0, :, 0:256], middle, second[:, 128:384]], axis=1)
    out_ref[...] = whole.astype(jnp.bfloat16).reshape(16, SIDE, 640)


def window_attend(shard, qkv, tables, select):
    spec = pltpu.PrefetchScalarGridSpec(
        num_scalar_prefetch=1,
        grid=(5, 2),
        in_specs=[
            pl.BlockSpec((2, 28, SIDE, 960), lambda w, p, s: (p, 0, w, 0)),
            pl.BlockSpec((256, 384), lambda w, p, s: (0, 0)),
            pl.BlockSpec((GROUP, KEYS, 256), lambda w, p, s: (0, 0, 0)),
        ],
        out_specs=pl.BlockSpec((16, SIDE, 640), lambda w, p, s: (0, w, p)),
        scratch_shapes=[pltpu.VMEM((2, 16 * SIDE, 384), jnp.float32)],
    )
    return pl.pallas_call(
        forward_kernel,
        grid_spec=spec,
        out_shape=jax.ShapeDtypeStruct((16, 5 * SIDE, 1280), jnp.bfloat16),
        compiler_params=pltpu.CompilerParams(vmem_limit_bytes=48 << 20),
        cost_estimate=pl.CostEstimate(flops=50_000_000_000, bytes_accessed=20_000_000, transcendentals=0),
        name="attend",
    )(shard, qkv, tables, select)


def backward_kernel(
    shard_ref, qkv_ref, grad_ref, table_ref, back_ref, select_ref, spread_ref, own_ref, other_ref, sums_ref, dq, dk, dv
):
    first = 2 * shard_ref[0]
    queries = 16 * SIDE

    @pl.when(pl.program_id(0) == 0)
    def _():
        sums_ref[...] = jnp.zeros_like(sums_ref)

    lane = lane_iota((SIDE, 128)) % 32
    for part, out_ref in enumerate((own_ref, other_ref)):
        q, k, v = load_group(qkv_ref, part, first)
        v = pad_lanes(v, 384)
        if part == 0:
            go = grad_ref[:, :, 0:384].reshape(queries, 384)
        else:
            go = shift_lanes(grad_ref[:, :, 256:640].reshape(queries, 384), -64).astype(jnp.bfloat16)
        q_sides = by_side(q, first)
        go_sides = by_side(go, first)
        bias = bias_rows(q, table_ref[...], first)
        dq[...] = jnp.zeros_like(dq)
        dk[...] = jnp.zeros_like(dk)
        dv[...] = jnp.zeros_like(dv)
        marks = jnp.zeros((queries, 128), jnp.float32)
        for head in range(GROUP):
            low, high = SLABS[head]
            keys = head_mask(k[:, low:high], head, low)
            values = head_mask(v[:, low:high], head, low)
            probs = softmax_rows(q_sides, keys, bias, select_ref[head], head)
            probs_low = probs.astype(jnp.bfloat16)
            go_both = beside(go_sides[0][:, low:high], go_sides[1][:, low:high])
            probs_grad = dot(go_both, beside(values[:KEYS], values[KEYS:]), NT)
            weighted = probs * probs_grad
            scores_grad = weighted - probs * jnp.sum(weighted, axis=1, keepdims=True)
            scores_low = scores_grad.astype(jnp.bfloat16)
            width = high - low
            go_head = beside(*(head_mask(side[:, low:high], head, low) for side in go_sides))
            q_head = beside(*(head_mask(side[:, low:high], head, low) for side in q_sides))
            value_grad = dot(probs_low, go_head, TN)
            key_grad = dot(scores_low, q_head, TN)
            for side in range(2):
                span = slice(side * KEYS, (side + 1) * KEYS)
                lanes = slice(side * width, (side + 1) * width)
                dv[span, low:high] += value_grad[:, lanes]
                dk[span, low:high] += key_grad[:, lanes]
            back = jnp.concatenate([keys[:KEYS], keys[KEYS:], spread_ref[head]], axis=1)
            joint = dot(scores_low, back, NN)
            dq[:, low:high] += pick_side(joint[:, :2 * width], first)
            marks = marks + joint[:, 2 * width:]
        highs, wides = [], []
        for row in range(16):
            ih = lax.rem(first + row, WIN)
            piece = marks[row * SIDE:(row + 1) * SIDE]
            highs.append(pltpu.roll(jnp.where(lane < 14, piece, 0.0), 13 - ih, 1))
            across = jnp.where((lane >= 16) & (lane < 30), piece, 0.0)
            wides.append(pltpu.roll(across, 112, 1, stride=1, stride_axis=0))
        ranks = jnp.concatenate([jnp.concatenate(highs), jnp.concatenate(wides)], axis=1).astype(jnp.bfloat16)
        dq_full = (dq[...] * SCALE + dot(ranks, back_ref[...], NN)).reshape(16, SIDE, 384)
        sums_ref[...] += dot(ranks, q, TN)
        dk_all = pltpu.roll(dk[...] * SCALE, 64, 1)
        joint = lane_iota((28 * SIDE, 128))
        middle = jnp.where(joint < 64, 0.0, dk_all[:, 0:128])
        right = jnp.concatenate([middle, dk_all[:, 128:384]], axis=1).reshape(28, SIDE, 384)
        out_ref[:, :, 0:256] = jnp.zeros((28, SIDE, 256), jnp.bfloat16)
        out_ref[:, :, 256:640] = right.astype(jnp.bfloat16)
        own_rows = pl.ds(first, 16)
        out_ref[own_rows, :, 0:256] = dq_full[:, :, 0:256].astype(jnp.bfloat16)
        edge = out_ref[own_rows, :, 256:384].astype(jnp.float32) + dq_full[:, :, 256:384]
        out_ref[own_rows, :, 256:384] = edge.astype(jnp.bfloat16)
        out_ref[:, :, 640:960] = dv[:, 0:320].astype(jnp.bfloat16).reshape(28, SIDE, 320)


def window_attend_back(pair, shard, qkv, grad, tables, back, select, spread):
    spec = pltpu.PrefetchScalarGridSpec(
        num_scalar_prefetch=1,
        grid=(5,),
        in_specs=[
            pl.BlockSpec((2, 28, SIDE, 960), lambda w, s: (pair, 0, w, 0)),
            pl.BlockSpec((16, SIDE, 640), lambda w, s: (0, w, pair)),
            pl.BlockSpec((256, 384), lambda w, s: (0, 0)),
            pl.BlockSpec((256, 384), lambda w, s: (0, 0)),
            pl.BlockSpec((GROUP, KEYS, 256), lambda w, s: (0, 0, 0)),
            pl.BlockSpec((GROUP, KEYS, 128), lambda w, s: (0, 0, 0)),
        ],
        out_specs=[
            pl.BlockSpec((28, SIDE, 960), lambda w, s: (0, w, 0)),
            pl.BlockSpec((28, SIDE, 960), lambda w, s: (0, w, 0)),
            pl.BlockSpec((256, 384), lambda w, s: (0, 0)),
        ],
        scratch_shapes=[
            pltpu.VMEM((16 * SIDE, 384), jnp.float32),
            pltpu.VMEM((2 * KEYS, 384), jnp.float32),
            pltpu.VMEM((2 * KEYS, 384), jnp.float32),
        ],
    )
    return pl.pallas_call(
        backward_kernel,
        grid_spec=spec,
        out_shape=[
            jax.ShapeDtypeStruct((28, 5 * SIDE, 960), jnp.bfloat16),
            jax.ShapeDtypeStruct((28, 5 * SIDE, 960), jnp.bfloat16),
            jax.ShapeDtypeStruct((256, 384), jnp.float32),
        ],
        compiler_params=pltpu.CompilerParams(vmem_limit_bytes=48 << 20),
        cost_estimate=pl.CostEstimate(flops=60_000_000_000, bytes_accessed=20_000_000, transcendentals=0),
        name="attend_back",
    )(shard, qkv, grad, tables, back, select, spread)


def project_kernel(shard_ref, x_ref, w_ref, bias_ref, out_ref, proj_ref):
    weights = w_ref[0][:, :960]
    for start in range(0, x_ref.shape[0], 448):
        rows = slice(start, start + 448)
        out_ref[0, rows, :] = (dot(x_ref[rows, :], weights, NN) + bias_ref[0]).astype(jnp.bfloat16)
    odd = pl.program_id(0) % 2

    @pl.when(odd == 0)
    def _():
        proj_ref[:, 0:384] = shift_lanes(w_ref[0, :, 896:1280], -64).astype(jnp.bfloat16)

    @pl.when(odd == 1)
    def _():
        lane = lane_iota((1, 128))
        left = (lane < 64).astype(jnp.float32).astype(jnp.bfloat16)
        right = (lane >= 64).astype(jnp.float32).astype(jnp.bfloat16)
        proj_ref[:, 256:384] = proj_ref[:, 256:384] * left + w_ref[0, :, 896:1024] * right
        proj_ref[:, 384:640] = w_ref[0, :, 1024:1280]


def project(shard, x, weights, bias):
    tokens, width = x.shape
    spec = pltpu.PrefetchScalarGridSpec(
        num_scalar_prefetch=1,
        grid=(4,),
        in_specs=[
            pl.BlockSpec((tokens, width), lambda p, s: (0, 0)),
            pl.BlockSpec((1, width, 1280), lambda p, s: (p ^ s[0], 0, 0)),
            pl.BlockSpec((1, 1, 960), lambda p, s: (p ^ s[0], 0, 0)),
        ],
        out_specs=[
            pl.BlockSpec((1, tokens, 960), lambda p, s: (p, 0, 0)),
            pl.BlockSpec((width, 640), lambda p, s: (0, p // 2)),
        ],
    )
    return pl.pallas_call(
        project_kernel,
        grid_spec=spec,
        out_shape=[
            jax.ShapeDtypeStruct((4, tokens, 960), jnp.bfloat16),
            jax.ShapeDtypeStruct((width, 1280), jnp.bfloat16),
        ],
        compiler_params=pltpu.CompilerParams(vmem_limit_bytes=48 << 20),
        cost_estimate=pl.CostEstimate(flops=24_000_000_000, bytes_accessed=35_000_000, transcendentals=0),
        name="project",
    )(shard, x, weights, bias)


def frame_kernel(shard_ref, near_own, near_other, far_own, far_other, w_ref, fold_ref, out_ref, sums_ref):
    total = None
    for p, back_ref in enumerate((near_own, near_other, far_own, far_other)):
        back = back_ref[...]
        piece = dot(back, w_ref[p ^ shard_ref[0]][:, :960], NT)
        total = piece if total is None else total + piece
        column = jnp.sum(back.astype(jnp.float32), axis=0, keepdims=True)

        @pl.when(pl.program_id(0) == 0)
        def _():
            sums_ref[p] = column

        @pl.when(pl.program_id(0) > 0)
        def _():
            sums_ref[p] += column
    total = total.astype(jnp.bfloat16)
    for row in range(out_ref.shape[0]):
        piece = total[row * 80:(row + 1) * 80, :]
        out_ref[row] = dot(fold_ref[...], piece, NN).astype(jnp.bfloat16)


def frame_back(shard, backs, weights, fold):
    width = weights.shape[1]
    chunk = 7
    back_spec = pl.BlockSpec((chunk * 80, 960), lambda g, s: (g, 0))
    spec = pltpu.PrefetchScalarGridSpec(
        num_scalar_prefetch=1,
        grid=(28 // chunk,),
        in_specs=[back_spec] * 4 + [
            pl.BlockSpec((4, width, 1280), lambda g, s: (0, 0, 0), pipeline_mode=pl.Buffered(1)),
            pl.BlockSpec(fold.shape, lambda g, s: (0, 0)),
        ],
        out_specs=[
            pl.BlockSpec((chunk, 64, width), lambda g, s: (g, 0, 0)),
            pl.BlockSpec((4, 1, 960), lambda g, s: (0, 0, 0)),
        ],
    )
    return pl.pallas_call(
        frame_kernel,
        grid_spec=spec,
        out_shape=[
            jax.ShapeDtypeStruct((28, 64, width), jnp.bfloat16),
            jax.ShapeDtypeStruct((4, 1, 960), jnp.float32),
        ],
        compiler_params=pltpu.CompilerParams(vmem_limit_bytes=58 << 20),
        cost_estimate=pl.CostEstimate(flops=1_000_000, bytes_accessed=1_000_000, transcendentals=0),
        name="frame_back",
    )(shard, *backs, weights, fold)


def turn_kernel(x_ref, out_ref):
    out_ref[...] = x_ref[...].T


def turn(x):
    return pl.pallas_call(
        turn_kernel,
        out_shape=jax.ShapeDtypeStruct(x.shape[::-1], x.dtype),
        compiler_params=pltpu.CompilerParams(vmem_limit_bytes=48 << 20),
        cost_estimate=pl.CostEstimate(flops=0, bytes_accessed=12_000_000, transcendentals=0),
        name="turn",
    )(x)


ROWS = 16
FRAME = 28
EARLY, LATE = 6, 12
EPSILON = 1e-06


def swap(values, shifts):
    return lax.ppermute(values, "tensor", shifts)


def own(values, index, axis=0):
    return lax.dynamic_index_in_dim(values, index, axis, keepdims=False)


def gather_small(values, shard):
    parts = [values]
    for step in (1, 2, 3):
        parts.append(swap(values, [(i, (i + step) % 4) for i in range(4)]))
    stack = jnp.stack(parts)
    return jnp.stack([own(stack, (shard - i) % 4) for i in range(4)])


CORES = [(0, 1), (1, 0), (2, 3), (3, 2)]
SIDES = [(0, 2), (2, 0), (1, 3), (3, 1)]


def add_low(left, right):
    return (left.astype(jnp.float32) + right.astype(jnp.float32)).astype(jnp.bfloat16)


def scatter_dp(quarter):
    return lax.psum_scatter(quarter, "dp", scatter_dimension=0, tiled=True)


def after(first, *values):
    return lax.optimization_barrier((first,) + values)[1:]


def sum_everywhere(values):
    values = values + swap(values, CORES)
    values = values + swap(values, SIDES)
    count = lax.axis_size("dp")
    step = 1
    while step < count:
        values = values + lax.ppermute(values, "dp", [(i, i ^ step) for i in range(count)])
        step *= 2
    return values


def statistics(values):
    average = jnp.mean(values, axis=-1, keepdims=True)
    centred = values - average
    rstd = lax.rsqrt(jnp.mean(centred * centred, axis=-1, keepdims=True) + EPSILON)
    return centred * rstd, rstd


def norm_back(grad, gain, hat, rstd):
    scaled = grad * gain
    mean_one = jnp.mean(scaled, axis=-1, keepdims=True)
    mean_two = jnp.mean(scaled * hat, axis=-1, keepdims=True)
    return rstd * (scaled - mean_one - hat * mean_two)


def column_selector():
    column = np.arange(GRID)
    place = SIDE * (column // WIN) + column % WIN
    select = np.zeros((NWIN * SIDE, GRID), np.float32)
    select[place, column] = 1.0
    return jnp.asarray(select, jnp.bfloat16)


def fast_shards(
    inputs,
    cotangent,
    teacher,
    qkv_weight,
    proj_weight,
    up_weight,
    down_weight,
    qv_bias,
    up_bias,
    norm_gains,
    norm_shifts,
    out_biases,
    rel_tables,
):
    f32, bf16 = jnp.float32, jnp.bfloat16
    shard = lax.axis_index("tensor")
    both = ("tensor", "dp")
    tokens = ROWS * GRID
    inner = qkv_weight.shape[1]
    joint = jnp.concatenate([qkv_weight.transpose(1, 0, 2).reshape(inner, 960), proj_weight.T], axis=1)
    joint = jnp.concatenate([joint, up_weight], axis=1)
    joint_all = lax.all_gather(joint, both, axis=0, tiled=True).reshape(4, D, 2560)
    biases = gather_small(jnp.concatenate([qv_bias.reshape(-1), up_bias]), shard)
    qkv_bias = jnp.concatenate(
        [biases[:, :320], jnp.zeros((4, 320), bf16), biases[:, 320:640]], axis=1
    ).astype(f32)
    up_bias_all = biases[:, 640:].astype(f32)

    gains = norm_gains.astype(f32)
    shifts = norm_shifts.astype(f32)
    image = inputs[0]
    above = swap(image[ROWS - EARLY:], [(i, i + 1) for i in range(3)])
    below = swap(image[:LATE], [(i + 1, i) for i in range(3)])
    framed = lax.dynamic_slice_in_dim(
        jnp.concatenate([above, image, below]), EARLY - 2 * shard, FRAME, 0
    )
    frame_hat, _ = statistics(framed.astype(f32))
    inside = (WIN * shard + jnp.arange(FRAME) < GRID)[:, None, None]
    normed = jnp.where(inside, frame_hat * gains[0] + shifts[0], 0.0).astype(bf16)
    select = column_selector()
    windows = jnp.einsum("pc,rcd->rpd", select, normed, preferred_element_type=f32).astype(bf16)
    flat = windows.reshape(FRAME * NWIN * SIDE, D)
    where = shard[None].astype(jnp.int32)
    qkv, proj_full = project(where, flat, joint_all, qkv_bias[:, None, :])
    qkv = qkv.reshape(4, FRAME, NWIN * SIDE, 960)
    tables, back_tables = bias_tables(rel_tables)
    select_keys, spread_keys = selectors()
    flat_turned = turn(flat)
    (down_shard,) = after((joint_all, flat_turned), down_weight.T)
    down_all = lax.all_gather(down_shard, both, axis=0, tiled=True).reshape(4, D, 1280)
    up_all = joint_all[:, :, 1280:]
    attended = window_attend(where, qkv, tables, select_keys)
    attended = jnp.einsum("pc,rpd->rcd", select, attended, preferred_element_type=f32)
    attended = attended.astype(bf16).reshape(tokens, D)

    source = image.astype(f32).reshape(tokens, D)
    branch = jnp.einsum("nk,ck->nc", attended, proj_full, preferred_element_type=f32)
    middle = source + branch + out_biases[0].astype(f32)
    second_hat, second_rstd = statistics(middle)
    normed_two = (second_hat * gains[1] + shifts[1]).astype(bf16)
    hidden = jnp.einsum("nd,tdm->tnm", normed_two, up_all, preferred_element_type=f32)
    hidden = hidden + up_bias_all[:, None, :]
    cdf = 0.5 + 0.5 * lax.erf(hidden * (0.5 ** 0.5))
    active = (hidden * cdf).astype(bf16)
    slope = (cdf + hidden * (jnp.exp(-0.5 * hidden * hidden) * (0.5 / np.pi) ** 0.5)).astype(bf16)
    result = jnp.einsum("tnm,tcm->nc", active, down_all, preferred_element_type=f32)
    result = middle + result + out_biases[1].astype(f32)
    mismatch = result - teacher[0].astype(f32).reshape(tokens, D)
    loss_total = jnp.sum(mismatch * mismatch)
    output = result.astype(bf16)

    result_grad = cotangent[0].astype(f32).reshape(tokens, D) + mismatch
    result_low = result_grad.astype(bf16)
    def down_block(p):
        return jnp.einsum("nc,nm->cm", result_low, own(active, shard ^ p), preferred_element_type=f32)

    sends = [down_block(3).astype(bf16), down_block(1).astype(bf16)]
    down_three, down_one = swap(sends[0], CORES), swap(sends[1], CORES)
    (result_next,) = after(tuple(sends), result_low)
    active_grad = jnp.einsum("nc,tcm->tnm", result_next, down_all, preferred_element_type=f32)
    hidden_grad = active_grad * slope.astype(f32)
    up_bias_acc = jnp.sum(hidden_grad, axis=1)
    hidden_low = hidden_grad.astype(bf16)
    down_far = (down_block(2) + down_three.astype(f32)).astype(bf16)
    down_near = (down_block(0) + down_one.astype(f32)).astype(bf16)
    down_side = swap(down_far, SIDES)
    hidden_low, normed_two = after((down_far, down_near), hidden_low, normed_two)

    def up_block(p):
        return jnp.einsum("nd,nm->dm", normed_two, own(hidden_low, shard ^ p), preferred_element_type=f32)

    sends = [up_block(3).astype(bf16), up_block(1).astype(bf16)]
    up_three, up_one = swap(sends[0], CORES), swap(sends[1], CORES)
    (hidden_next,) = after(tuple(sends), hidden_low)
    second_grad = jnp.einsum("tnm,tdm->nd", hidden_next, up_all, preferred_element_type=f32)
    middle_grad = result_grad + norm_back(second_grad, gains[1], second_hat, second_rstd)
    second_gain = jnp.sum(second_grad * second_hat, axis=0)
    second_shift = jnp.sum(second_grad, axis=0)
    middle_low = middle_grad.astype(bf16)
    attended_grad = jnp.einsum("nc,ck->nk", middle_low, proj_full, preferred_element_type=f32)
    attended_grad = attended_grad.astype(bf16).reshape(ROWS, GRID, D)
    attended_grad = jnp.einsum("pc,rcd->rpd", select, attended_grad, preferred_element_type=f32)
    attended_grad = attended_grad.astype(bf16)
    up_far = (up_block(2) + up_three.astype(f32)).astype(bf16)
    up_near = (up_block(0) + up_one.astype(f32)).astype(bf16)
    up_side = swap(up_far, SIDES)

    def proj_block(p):
        part = attended[:, 320 * p:320 * p + 320]
        return jnp.einsum("nc,nk->ck", middle_low, part, preferred_element_type=f32)

    proj_sends = (proj_block(3).astype(bf16), proj_block(1).astype(bf16))
    proj_three, proj_one = swap(proj_sends[0], CORES), swap(proj_sends[1], CORES)
    (down_near,) = after((up_far, up_near, proj_sends), down_near)
    down_quarter = add_low(down_near, down_side)
    (grad_far,) = after((up_far, up_near, down_quarter), attended_grad)
    far_own, far_other, far_sums = window_attend_back(
        1, where, qkv, grad_far, tables, back_tables, select_keys, spread_keys
    )

    def flatten(back):
        return back.reshape(FRAME * NWIN * SIDE, 960)

    def qkv_block(tokens_in, back):
        return jnp.einsum("dn,nc->dc", tokens_in, back, preferred_element_type=f32)

    far_own, far_other = flatten(far_own), flatten(far_other)
    qkv_send = qkv_block(flat_turned, far_other).astype(bf16)
    qkv_three = swap(qkv_send, CORES)
    flat_far, up_side, _ = lax.optimization_barrier((flat_turned, up_side, qkv_send))
    up_quarter = add_low(up_near, up_side)
    mlp_grad = scatter_dp(jnp.concatenate([up_quarter, down_quarter], axis=1))
    proj_far = (proj_block(2) + proj_three.astype(f32)).astype(bf16)
    proj_near = (proj_block(0) + proj_one.astype(f32)).astype(bf16)
    qkv_far = (qkv_block(flat_far, far_own) + qkv_three.astype(f32)).astype(bf16)
    far_side = swap(jnp.concatenate([qkv_far, proj_far], axis=1), SIDES)
    (grad_near,) = after((qkv_far, proj_far, proj_near, up_quarter), attended_grad)
    near_own, near_other, near_sums = window_attend_back(
        0, where, qkv, grad_near, tables, back_tables, select_keys, spread_keys
    )
    near_own, near_other = flatten(near_own), flatten(near_other)
    qkv_send = qkv_block(flat_turned, near_other).astype(bf16)
    qkv_one = swap(qkv_send, CORES)
    backs = after(qkv_send, near_own, near_other, far_own, far_other)
    frame_grad, bias_sums = frame_back(where, backs, joint_all, select.T)
    flat_near, far_side, _ = lax.optimization_barrier((flat_turned, far_side, frame_grad))
    qkv_near = qkv_block(flat_near, near_own) + qkv_one.astype(f32)
    near = jnp.concatenate([qkv_near.astype(bf16), proj_near], axis=1)
    joint_quarter = add_low(near, far_side)
    mlp_grad, joint_ready = lax.optimization_barrier((mlp_grad, joint_quarter))
    joint_grad = scatter_dp(joint_ready)
    table_sums = far_sums + near_sums
    (frame_grad,) = after(joint_quarter, frame_grad)
    bias_sums = bias_sums[:, 0]
    qv_acc = jnp.stack([bias_sums[:, :320], bias_sums[:, 640:]], axis=1)
    qv_acc = jnp.stack([own(qv_acc, shard ^ t) for t in range(4)])
    table_sums = table_sums[:, :320].reshape(2, GROUP, 32, GROUP, HEAD_DIM)
    table_acc = jnp.einsum("phrhd->prd", table_sums)
    table_acc = jnp.stack([table_acc[0, :27][::-1], table_acc[1, :27]])
    spread = jnp.zeros((EARLY + ROWS + LATE, GRID, D), bf16)
    spread = lax.dynamic_update_slice_in_dim(spread, frame_grad, EARLY - 2 * shard, 0)
    from_next = swap(spread[:EARLY], [(i + 1, i) for i in range(3)])
    from_before = swap(spread[EARLY + ROWS:], [(i, i + 1) for i in range(3)])
    first_grad = spread[EARLY:EARLY + ROWS].astype(f32)
    first_grad = first_grad + jnp.pad(from_next.astype(f32), ((ROWS - EARLY, 0), (0, 0), (0, 0)))
    first_grad = first_grad + jnp.pad(from_before.astype(f32), ((0, ROWS - LATE), (0, 0), (0, 0)))
    first_grad = first_grad.reshape(tokens, D)
    first_hat, first_rstd = statistics(source)
    first_gain = jnp.sum(first_grad * first_hat, axis=0)
    first_shift = jnp.sum(first_grad, axis=0)
    input_grad = middle_grad + norm_back(first_grad, gains[0], first_hat, first_rstd)

    small = [
        qv_acc, up_bias_acc, first_gain, second_gain, first_shift, second_shift,
        jnp.sum(middle_grad, axis=0), jnp.sum(result_grad, axis=0), table_acc, loss_total,
    ]
    sums = sum_everywhere(jnp.concatenate([part.reshape(-1) for part in small]))
    parts = []
    place = 0
    for part in small:
        parts.append(sums[place:place + part.size].reshape(part.shape))
        place += part.size
    qv_sum, up_sum, gain_one, gain_two, shift_one, shift_two, bias_one, bias_two, table_grad, loss_sum = parts
    loss = loss_sum / (tokens * D * lax.axis_size("dp") * lax.axis_size("tensor"))
    return (
        output.reshape(1, ROWS, GRID, D),
        input_grad.reshape(1, ROWS, GRID, D),
        loss,
        joint_grad[:, :960].reshape(inner, 3, 320).transpose(1, 0, 2).astype(f32),
        joint_grad[:, 960:].T.astype(f32),
        mlp_grad[:, :1280].astype(f32),
        mlp_grad[:, 1280:].T.astype(f32),
        own(qv_sum, shard),
        own(up_sum, shard),
        jnp.stack([gain_one, gain_two]),
        jnp.stack([shift_one, shift_two]),
        jnp.stack([bias_one, bias_two]),
        table_grad,
    )


def solution(mesh):
    in_specs = (
        P("dp", "tensor", None, None),
        P("dp", "tensor", None, None),
        P("dp", "tensor", None, None),
        P(None, "dp", "tensor"),
        P("tensor", "dp"),
        P("dp", "tensor"),
        P("tensor", "dp"),
        P(None, "tensor"),
        P("tensor"),
        P(),
        P(),
        P(),
        P(),
    )
    out_specs = (
        P("dp", "tensor", None, None),
        P("dp", "tensor", None, None),
        P(),
        P(None, "dp", "tensor"),
        P("tensor", "dp"),
        P("dp", "tensor"),
        P("tensor", "dp"),
        P(None, "tensor"),
        P("tensor"),
        P(),
        P(),
        P(),
        P(),
    )
    fits = mesh.shape["tensor"] == 4 and GRID // mesh.shape["tensor"] == 16
    shards = fast_shards if fits else general_shards
    return jax.shard_map(shards, mesh=mesh, in_specs=in_specs, out_specs=out_specs, check_vma=False)
```

```python
from functools import partial

import jax
import jax.numpy as jnp
import numpy as np
from jax import lax
from jax.experimental import pallas as pl
from jax.experimental.pallas import tpu as pltpu
from jax.sharding import PartitionSpec as P

D = 1280
HEAD_DIM = 80
GRID = 64
WIN = 14
PGRID = 70
NWIN = 5


highest = lax.Precision.HIGHEST


def layer_norm(values, gain_vector, shift_vector):
    average = jnp.mean(values, axis=-1, keepdims=True)
    centred = values - average
    variance = jnp.mean(centred * centred, axis=-1, keepdims=True)
    return centred * lax.rsqrt(variance + 1e-06) * gain_vector + shift_vector


def exact_gelu(values):
    return jax.nn.gelu(values, approximate=False)


def offset_tables(window):
    position = jnp.arange(window * window)
    across = jnp.arange(window)
    ranks = jnp.arange(2 * window - 1)
    high_sel = (
        position[:, None, None] // window - across[None, :, None] + window - 1
        == ranks[None, None, :]
    ).astype(jnp.float32)
    wide_sel = (
        position[:, None, None] % window - across[None, :, None] + window - 1
        == ranks[None, None, :]
    ).astype(jnp.float32)
    return (high_sel, wide_sel)


def to_windows(grid_values):
    extra = PGRID - GRID
    padded = jnp.pad(grid_values, ((0, extra), (0, extra), (0, 0)))
    channels = grid_values.shape[-1]
    shaped = padded.reshape(NWIN, WIN, NWIN, WIN, channels).transpose(0, 2, 1, 3, 4)
    return shaped.reshape(NWIN, NWIN, WIN * WIN, channels)


def from_windows(windowed):
    channels = windowed.shape[-1]
    shaped = windowed.reshape(NWIN, NWIN, WIN, WIN, channels).transpose(0, 2, 1, 3, 4)
    return shaped.reshape(PGRID, PGRID, channels)[:GRID, :GRID]


def score_block(queries, key_rows, tables, selectors):
    table_high, table_wide = tables
    high_sel, wide_sel = selectors
    raw = jnp.einsum(
        "wqhc,wkhc->whqk", queries, key_rows, preferred_element_type=jnp.float32
    ) * HEAD_DIM ** (-0.5)
    along_high = jnp.einsum(
        "wqhc,rc->wqhr", queries, table_high, preferred_element_type=jnp.float32
    )
    along_wide = jnp.einsum(
        "wqhc,rc->wqhr", queries, table_wide, preferred_element_type=jnp.float32
    )
    bias_high = jnp.einsum("wqhr,qkr->whqk", along_high, high_sel, precision=highest)
    bias_wide = jnp.einsum("wqhr,qkr->whqk", along_wide, wide_sel, precision=highest)
    shaped = (
        raw.reshape(raw.shape[:3] + (WIN, WIN)) + bias_high[..., :, None] + bias_wide[..., None, :]
    )
    return shaped.reshape(raw.shape)


def attend_row(block_parts, tables, selectors):
    queries, key_rows, value_rows = block_parts
    scores = score_block(queries, key_rows, tables, selectors)
    row_max = jnp.max(scores, axis=-1, keepdims=True)
    shifted = jnp.exp(scores - row_max)
    row_total = jnp.sum(shifted, axis=-1, keepdims=True)
    probs_low = (shifted / row_total).astype(jnp.bfloat16)
    attended = jnp.einsum(
        "whqk,wkhc->wqhc", probs_low, value_rows, preferred_element_type=jnp.float32
    )
    return (attended.astype(jnp.bfloat16), (row_max + jnp.log(row_total))[..., 0])


def attend_back(block_parts, tables, selectors):
    queries, key_rows, value_rows, attended_grad, log_total = block_parts
    high_sel, wide_sel = selectors
    scores = score_block(queries, key_rows, tables, selectors)
    probs = jnp.exp(scores - log_total[..., None])
    probs_grad = jnp.einsum(
        "wqhc,wkhc->whqk", attended_grad, value_rows, preferred_element_type=jnp.float32
    )
    value_grad = jnp.einsum(
        "whqk,wqhc->wkhc",
        probs.astype(jnp.bfloat16),
        attended_grad,
        preferred_element_type=jnp.float32,
    )
    scores_grad = probs * (probs_grad - jnp.sum(probs * probs_grad, axis=-1, keepdims=True))
    scores_low = scores_grad.astype(jnp.bfloat16)
    query_grad = jnp.einsum(
        "whqk,wkhc->wqhc", scores_low, key_rows, preferred_element_type=jnp.float32
    ) * HEAD_DIM ** (-0.5)
    key_grad = jnp.einsum(
        "whqk,wqhc->wkhc", scores_low, queries, preferred_element_type=jnp.float32
    ) * HEAD_DIM ** (-0.5)
    shaped = scores_grad.reshape(scores_grad.shape[:3] + (WIN, WIN))
    rank_high = jnp.einsum("whqa,qar->wqhr", jnp.sum(shaped, axis=-1), high_sel, precision=highest)
    rank_wide = jnp.einsum("whqb,qbr->wqhr", jnp.sum(shaped, axis=-2), wide_sel, precision=highest)
    table_high = tables[0].astype(jnp.float32)
    table_wide = tables[1].astype(jnp.float32)
    query_grad = query_grad + jnp.einsum("wqhr,rc->wqhc", rank_high, table_high, precision=highest)
    query_grad = query_grad + jnp.einsum("wqhr,rc->wqhc", rank_wide, table_wide, precision=highest)
    query_wide = queries.astype(jnp.float32)
    table_grad = jnp.stack(
        [
            jnp.einsum("wqhr,wqhc->rc", rank_high, query_wide, precision=highest),
            jnp.einsum("wqhr,wqhc->rc", rank_wide, query_wide, precision=highest),
        ]
    )
    return (query_grad, key_grad, value_grad, table_grad)


def general_shards(
    inputs,
    cotangent,
    teacher,
    qkv_weight,
    proj_weight,
    up_weight,
    down_weight,
    qv_bias,
    up_bias,
    norm_gains,
    norm_shifts,
    out_biases,
    rel_tables,
):
    qkv_full, proj_full, up_full, down_full = (
        lax.all_gather(qkv_weight, "dp", axis=1, tiled=True),
        lax.all_gather(proj_weight, "dp", axis=1, tiled=True),
        lax.all_gather(up_weight, "dp", axis=0, tiled=True),
        lax.all_gather(down_weight, "dp", axis=1, tiled=True),
    )
    up_matrix, down_matrix, up_bias_all = (up_full, down_full, up_bias)
    images, row_count = (inputs.shape[0], inputs.shape[1])
    local_width = qkv_full.shape[2]
    head_count = local_width // HEAD_DIM
    head_shape = (NWIN, NWIN, WIN * WIN, head_count, HEAD_DIM)
    selectors = offset_tables(WIN)
    tables = (rel_tables[0], rel_tables[1])
    gains_wide = norm_gains.astype(jnp.float32)
    shifts_wide = norm_shifts.astype(jnp.float32)
    source = inputs[0].astype(jnp.float32)
    normed = layer_norm(source, gains_wide[0], shifts_wide[0]).astype(jnp.bfloat16)
    gathered = lax.all_gather(normed, "tensor", axis=0, tiled=True)
    windows = to_windows(gathered)
    projected = jnp.einsum("abpd,sdc->sabpc", windows, qkv_full, preferred_element_type=jnp.float32)
    queries = (projected[0] + qv_bias[0]).astype(jnp.bfloat16).reshape(head_shape)
    key_rows = projected[1].astype(jnp.bfloat16).reshape(head_shape)
    value_rows = (projected[2] + qv_bias[1]).astype(jnp.bfloat16).reshape(head_shape)
    attended, log_totals = lax.map(
        partial(attend_row, tables=tables, selectors=selectors), (queries, key_rows, value_rows)
    )
    grid_out = from_windows(attended.reshape(NWIN, NWIN, WIN * WIN, local_width))
    row_piece = grid_out
    attn_branch = lax.psum_scatter(
        jnp.einsum("xyc,cd->xyd", row_piece, proj_full, preferred_element_type=jnp.float32).astype(
            jnp.bfloat16
        ),
        "tensor",
        scatter_dimension=0,
        tiled=True,
    ).astype(jnp.float32)
    middle = source + attn_branch + out_biases[0].astype(jnp.float32)
    normed_two = layer_norm(middle, gains_wide[1], shifts_wide[1]).astype(jnp.bfloat16)
    mlp_input = lax.all_gather(normed_two, "tensor", axis=0, tiled=True)
    hidden = (
        jnp.einsum("xyd,dm->xym", mlp_input, up_matrix, preferred_element_type=jnp.float32)
        + up_bias_all
    )
    active = exact_gelu(hidden).astype(jnp.bfloat16)
    row_piece = active
    mlp_branch = lax.psum_scatter(
        jnp.einsum(
            "xym,md->xyd", row_piece, down_matrix, preferred_element_type=jnp.float32
        ).astype(jnp.bfloat16),
        "tensor",
        scatter_dimension=0,
        tiled=True,
    ).astype(jnp.float32)
    result = middle + mlp_branch + out_biases[1].astype(jnp.float32)
    mismatch = result - teacher[0].astype(jnp.float32)
    loss_total = jnp.sum(mismatch * mismatch)
    outputs = [result.astype(jnp.bfloat16)]
    result_grad = cotangent[0].astype(jnp.float32) + mismatch
    result_low = result_grad.astype(jnp.bfloat16)
    grad_rows = lax.all_gather(result_low, "tensor", axis=0, tiled=True)
    down_acc = jnp.einsum("xym,xyd->md", active, grad_rows, preferred_element_type=jnp.float32)
    active_grad = jnp.einsum(
        "xyd,md->xym", grad_rows, down_matrix, preferred_element_type=jnp.float32
    )
    gelu_value, gelu_back = jax.vjp(exact_gelu, hidden)
    hidden_grad = gelu_back(active_grad)[0]
    up_bias_acc = jnp.sum(hidden_grad, axis=(0, 1))
    hidden_low = hidden_grad.astype(jnp.bfloat16)
    up_acc = jnp.einsum("xyd,xym->dm", mlp_input, hidden_low, preferred_element_type=jnp.float32)
    row_piece = hidden_low
    second_grad = lax.psum_scatter(
        jnp.einsum("xym,dm->xyd", row_piece, up_matrix, preferred_element_type=jnp.float32).astype(
            jnp.bfloat16
        ),
        "tensor",
        scatter_dimension=0,
        tiled=True,
    ).astype(jnp.float32)
    second_value, second_back = jax.vjp(layer_norm, middle, gains_wide[1], shifts_wide[1])
    middle_part, second_gain, second_shift = second_back(second_grad)
    middle_grad = result_grad + middle_part
    out_bias_acc = jnp.stack([jnp.sum(middle_grad, axis=(0, 1)), jnp.sum(result_grad, axis=(0, 1))])
    middle_low = middle_grad.astype(jnp.bfloat16)
    gathered_grad = lax.all_gather(middle_low, "tensor", axis=0, tiled=True)
    proj_acc = jnp.einsum(
        "xyc,xyd->cd", grid_out, gathered_grad, preferred_element_type=jnp.float32
    )
    attended_grad = jnp.einsum(
        "xyd,cd->xyc", gathered_grad, proj_full, preferred_element_type=jnp.float32
    ).astype(jnp.bfloat16)
    grad_windows = to_windows(attended_grad).reshape(head_shape)
    query_grad, key_grad, value_grad, table_parts = lax.map(
        partial(attend_back, tables=tables, selectors=selectors),
        (queries, key_rows, value_rows, grad_windows, log_totals),
    )
    table_acc = jnp.sum(table_parts, axis=0)
    query_flat = query_grad.reshape(NWIN, NWIN, WIN * WIN, local_width)
    key_flat = key_grad.reshape(NWIN, NWIN, WIN * WIN, local_width)
    value_flat = value_grad.reshape(NWIN, NWIN, WIN * WIN, local_width)
    qv_acc = jnp.stack([jnp.sum(query_flat, axis=(0, 1, 2)), jnp.sum(value_flat, axis=(0, 1, 2))])
    stacked = jnp.stack([query_flat, key_flat, value_flat]).astype(jnp.bfloat16)
    qkv_acc = jnp.einsum("abpd,sabpc->sdc", windows, stacked, preferred_element_type=jnp.float32)
    normed_back = jnp.einsum(
        "sabpc,sdc->abpd", stacked, qkv_full, preferred_element_type=jnp.float32
    )
    first_grad = lax.psum_scatter(
        from_windows(normed_back).astype(jnp.bfloat16), "tensor", scatter_dimension=0, tiled=True
    ).astype(jnp.float32)
    first_value, first_back = jax.vjp(layer_norm, source, gains_wide[0], shifts_wide[0])
    source_part, first_gain, first_shift = first_back(first_grad)
    gain_acc = jnp.stack([first_gain, second_gain])
    shift_acc = jnp.stack([first_shift, second_shift])
    input_grads = [middle_grad + source_part]
    qkv_grad, proj_grad, up_grad, down_grad = (
        lax.psum_scatter(
            qkv_acc.astype(jnp.bfloat16), "dp", scatter_dimension=1, tiled=True
        ).astype(jnp.float32),
        lax.psum_scatter(
            proj_acc.astype(jnp.bfloat16), "dp", scatter_dimension=1, tiled=True
        ).astype(jnp.float32),
        lax.psum_scatter(up_acc.astype(jnp.bfloat16), "dp", scatter_dimension=0, tiled=True).astype(
            jnp.float32
        ),
        lax.psum_scatter(
            down_acc.astype(jnp.bfloat16), "dp", scatter_dimension=1, tiled=True
        ).astype(jnp.float32),
    )
    qv_grad, up_bias_grad = lax.psum((qv_acc, up_bias_acc), "dp")
    gains_grad, shifts_grad, out_grad, table_grad, loss_sum = lax.psum(
        (gain_acc, shift_acc, out_bias_acc, table_acc, loss_total), ("dp", "tensor")
    )
    element_count = images * row_count * GRID * D * lax.axis_size("dp") * lax.axis_size("tensor")
    loss = loss_sum / element_count
    return (
        jnp.stack(outputs),
        jnp.stack(input_grads),
        loss,
        qkv_grad,
        proj_grad,
        up_grad,
        down_grad,
        qv_grad,
        up_bias_grad,
        gains_grad,
        shifts_grad,
        out_grad,
        table_grad,
    )


SIDE = 16
GROUP = 4
KEYS = WIN * SIDE
SLABS = ((0, 128), (0, 256), (128, 256), (128, 384))
SCALE = HEAD_DIM ** (-0.5)
LOG2E = 1.4426950408889634
NT = (((1,), (1,)), ((), ()))
TN = (((0,), (0,)), ((), ()))
NN = (((1,), (0,)), ((), ()))


def dot(a, b, dims):
    return lax.dot_general(a, b, dims, preferred_element_type=jnp.float32)


def bias_tables(rel_tables):
    tables = rel_tables.astype(jnp.bfloat16)

    def place(rows):
        padded = jnp.pad(rows, ((0, 5), (0, 0)))
        eye = jnp.eye(GROUP, dtype=jnp.bfloat16)
        spread = eye[:, None, :, None] * padded[None, :, None, :]
        return spread.reshape(GROUP * 32, GROUP * HEAD_DIM)

    forward = jnp.concatenate([place(tables[0][::-1]), place(tables[1][::-1])])
    backward = jnp.concatenate([place(tables[0][::-1]), place(tables[1])])
    lanes = ((0, 0), (0, 64))
    return jnp.pad(forward, lanes), jnp.pad(backward, lanes)


def selectors():
    key = np.arange(KEYS)
    high, wide = key // SIDE, key % SIDE
    fwd = np.zeros((GROUP, KEYS, 128), np.float32)
    bwd = np.zeros((GROUP, KEYS, 128), np.float32)
    real = wide < WIN
    for head in range(GROUP):
        for j in range(KEYS):
            if real[j]:
                fwd[head, j, 32 * head + high[j]] = 1.0
                fwd[head, j, 32 * head + 16 + wide[j]] = 1.0
                bwd[head, j, 32 * head + high[j]] = 1.0
                bwd[head, j, 32 * head + 16 + 13 - wide[j]] = 1.0
            else:
                fwd[head, j, 32 * head + 14] = -1e30
    fwd = np.concatenate([fwd, fwd], axis=-1)
    return jnp.asarray(fwd, jnp.bfloat16), jnp.asarray(bwd, jnp.bfloat16)


def lane_iota(shape):
    return lax.broadcasted_iota(jnp.int32, shape, 1)


def head_mask(values, head, low):
    lane = lane_iota((1, values.shape[1])) + low
    inside = (lane >= HEAD_DIM * head) & (lane < HEAD_DIM * head + HEAD_DIM)
    return values * inside.astype(jnp.float32).astype(jnp.bfloat16)


def shift_lanes(values, amount):
    wide = values.astype(jnp.float32)
    return pltpu.roll(wide, amount % wide.shape[1], 1)


def load_group(qkv_ref, part, first):
    rows = qkv_ref.shape[1]
    q = qkv_ref[part, pl.ds(first, 16), :, 0:384].reshape(16 * SIDE, 384)
    k = qkv_ref[part, :, :, 256:640].reshape(rows * SIDE, 384)
    k = shift_lanes(k, -64).astype(jnp.bfloat16)
    v = qkv_ref[part, :, :, 640:960].reshape(rows * SIDE, 320)
    return q, k, v


def by_side(values, first):
    row = lax.broadcasted_iota(jnp.int32, (16 * SIDE, 1), 0)
    upper = (row < (WIN - first) * SIDE).astype(jnp.float32)
    return values * upper.astype(jnp.bfloat16), values * (1.0 - upper).astype(jnp.bfloat16)


def bias_rows(q, tables, first):
    along = dot(q, tables, NT) * (HEAD_DIM ** 0.5)
    high, wide = along[:, :128], along[:, 128:]
    pieces = []
    lane = lane_iota((SIDE, 128)) % 32
    for row in range(16):
        ih = lax.rem(first + row, WIN)
        rows = slice(row * SIDE, (row + 1) * SIDE)
        up = pltpu.roll(high[rows], lax.rem(ih + 115, 128), 1)
        across = pltpu.roll(wide[rows], 3, 1, stride=1, stride_axis=0)
        both = jnp.where(lane < 16, up, across)
        pieces.append(jnp.where(lane == 14, 1.0, both))
    both = jnp.concatenate(pieces)
    upper = both.astype(jnp.bfloat16)
    lower = (both - upper.astype(jnp.float32)).astype(jnp.bfloat16)
    return jnp.concatenate([upper, lower], axis=1)


def beside(upper, lower):
    return jnp.concatenate([upper, lower], axis=1)


def score_rows(q_sides, keys, bias, select, head):
    low, high = SLABS[head]
    left = jnp.concatenate([q_sides[0][:, low:high], q_sides[1][:, low:high], bias], axis=1)
    right = jnp.concatenate([keys[:KEYS], keys[KEYS:], select], axis=1)
    return dot(left, right, NT)


def softmax_rows(scores):
    top = jnp.max(scores, axis=1, keepdims=True)
    raised = jnp.exp2((scores - top) * (SCALE * LOG2E))
    total = jnp.sum(raised, axis=1, keepdims=True)
    return raised * (1.0 / total)


def pick_side(both, first):
    width = both.shape[1] // 2
    row = lax.broadcasted_iota(jnp.int32, (16 * SIDE, 1), 0)
    return jnp.where(row < (WIN - first) * SIDE, both[:, :width], both[:, width:])


def pad_lanes(values, width):
    missing = width - values.shape[1]
    if missing == 0:
        return values
    return jnp.concatenate([values, jnp.zeros((values.shape[0], missing), values.dtype)], axis=1)


def forward_kernel(shard_ref, qkv_ref, table_ref, select_ref, out_ref, acc):
    first = 2 * shard_ref[0]
    for part in range(2):
        q, k, v = load_group(qkv_ref, part, first)
        q_sides = by_side(q, first)
        bias = bias_rows(q, table_ref[...], first)
        v = pad_lanes(v, 384)
        scores = []
        for head in range(GROUP):
            low, high = SLABS[head]
            keys = head_mask(k[:, low:high], head, low)
            scores.append(score_rows(q_sides, keys, bias, select_ref[head], head))
        all_probs = [softmax_rows(rows).astype(jnp.bfloat16) for rows in scores]
        for head in range(GROUP):
            low, high = SLABS[head]
            probs = all_probs[head]
            values = head_mask(v[:, low:high], head, low)
            piece = pick_side(dot(probs, beside(values[:KEYS], values[KEYS:]), NN), first)
            if head == 0:
                acc[part, :, 0:128] = piece
                acc[part, :, 128:384] = jnp.zeros((16 * SIDE, 256), jnp.float32)
            else:
                acc[part, :, low:high] += piece
    second = pltpu.roll(acc[1], 64, 1)
    middle = acc[0, :, 256:384] + second[:, 0:128]
    whole = jnp.concatenate([acc[0, :, 0:256], middle, second[:, 128:384]], axis=1)
    out_ref[...] = whole.astype(jnp.bfloat16).reshape(16, SIDE, 640)


def window_attend(shard, qkv, tables, select):
    spec = pltpu.PrefetchScalarGridSpec(
        num_scalar_prefetch=1,
        grid=(5, 2),
        in_specs=[
            pl.BlockSpec((2, 28, SIDE, 960), lambda w, p, s: (p, 0, w, 0)),
            pl.BlockSpec((256, 384), lambda w, p, s: (0, 0)),
            pl.BlockSpec((GROUP, KEYS, 256), lambda w, p, s: (0, 0, 0)),
        ],
        out_specs=pl.BlockSpec((16, SIDE, 640), lambda w, p, s: (0, w, p)),
        scratch_shapes=[pltpu.VMEM((2, 16 * SIDE, 384), jnp.float32)],
    )
    return pl.pallas_call(
        forward_kernel,
        grid_spec=spec,
        out_shape=jax.ShapeDtypeStruct((16, 5 * SIDE, 1280), jnp.bfloat16),
        compiler_params=pltpu.CompilerParams(vmem_limit_bytes=48 << 20),
        cost_estimate=pl.CostEstimate(flops=50_000_000_000, bytes_accessed=20_000_000, transcendentals=0),
        name="attend",
    )(shard, qkv, tables, select)


def backward_kernel(
    shard_ref, qkv_ref, grad_ref, table_ref, back_ref, select_ref, spread_ref, own_ref, other_ref, sums_ref, dq, dk, dv
):
    first = 2 * shard_ref[0]
    queries = 16 * SIDE

    @pl.when(pl.program_id(0) == 0)
    def _():
        sums_ref[...] = jnp.zeros_like(sums_ref)

    lane = lane_iota((SIDE, 128)) % 32
    for part, out_ref in enumerate((own_ref, other_ref)):
        q, k, v = load_group(qkv_ref, part, first)
        v = pad_lanes(v, 384)
        if part == 0:
            go = grad_ref[:, :, 0:384].reshape(queries, 384)
        else:
            go = shift_lanes(grad_ref[:, :, 256:640].reshape(queries, 384), -64).astype(jnp.bfloat16)
        q_sides = by_side(q, first)
        go_sides = by_side(go, first)
        bias = bias_rows(q, table_ref[...], first)
        dq[...] = jnp.zeros_like(dq)
        dk[...] = jnp.zeros_like(dk)
        dv[...] = jnp.zeros_like(dv)
        marks = jnp.zeros((queries, 128), jnp.float32)
        all_keys, scores, grads = [], [], []
        for head in range(GROUP):
            low, high = SLABS[head]
            keys = head_mask(k[:, low:high], head, low)
            values = head_mask(v[:, low:high], head, low)
            all_keys.append(keys)
            scores.append(score_rows(q_sides, keys, bias, select_ref[head], head))
            go_both = beside(go_sides[0][:, low:high], go_sides[1][:, low:high])
            grads.append(dot(go_both, beside(values[:KEYS], values[KEYS:]), NT))
        for head in range(GROUP):
            low, high = SLABS[head]
            keys, probs_grad = all_keys[head], grads[head]
            probs = softmax_rows(scores[head])
            probs_low = probs.astype(jnp.bfloat16)
            weighted = probs * probs_grad
            scores_grad = weighted - probs * jnp.sum(weighted, axis=1, keepdims=True)
            scores_low = scores_grad.astype(jnp.bfloat16)
            width = high - low
            go_head = beside(*(head_mask(side[:, low:high], head, low) for side in go_sides))
            q_head = beside(*(head_mask(side[:, low:high], head, low) for side in q_sides))
            value_grad = dot(probs_low, go_head, TN)
            key_grad = dot(scores_low, q_head, TN)
            for side in range(2):
                span = slice(side * KEYS, (side + 1) * KEYS)
                lanes = slice(side * width, (side + 1) * width)
                dv[span, low:high] += value_grad[:, lanes]
                dk[span, low:high] += key_grad[:, lanes]
            back = jnp.concatenate([keys[:KEYS], keys[KEYS:], spread_ref[head]], axis=1)
            joint = dot(scores_low, back, NN)
            dq[:, low:high] += pick_side(joint[:, :2 * width], first)
            marks = marks + joint[:, 2 * width:]
        highs, wides = [], []
        for row in range(16):
            ih = lax.rem(first + row, WIN)
            piece = marks[row * SIDE:(row + 1) * SIDE]
            highs.append(pltpu.roll(jnp.where(lane < 14, piece, 0.0), 13 - ih, 1))
            across = jnp.where((lane >= 16) & (lane < 30), piece, 0.0)
            wides.append(pltpu.roll(across, 112, 1, stride=1, stride_axis=0))
        ranks = jnp.concatenate([jnp.concatenate(highs), jnp.concatenate(wides)], axis=1).astype(jnp.bfloat16)
        dq_full = (dq[...] * SCALE + dot(ranks, back_ref[...], NN)).reshape(16, SIDE, 384)
        sums_ref[...] += dot(ranks, q, TN)
        dk_all = pltpu.roll(dk[...] * SCALE, 64, 1)
        joint = lane_iota((28 * SIDE, 128))
        middle = jnp.where(joint < 64, 0.0, dk_all[:, 0:128])
        right = jnp.concatenate([middle, dk_all[:, 128:384]], axis=1).reshape(28, SIDE, 384)
        out_ref[:, :, 0:256] = jnp.zeros((28, SIDE, 256), jnp.bfloat16)
        out_ref[:, :, 256:640] = right.astype(jnp.bfloat16)
        own_rows = pl.ds(first, 16)
        out_ref[own_rows, :, 0:256] = dq_full[:, :, 0:256].astype(jnp.bfloat16)
        edge = out_ref[own_rows, :, 256:384].astype(jnp.float32) + dq_full[:, :, 256:384]
        out_ref[own_rows, :, 256:384] = edge.astype(jnp.bfloat16)
        out_ref[:, :, 640:960] = dv[:, 0:320].astype(jnp.bfloat16).reshape(28, SIDE, 320)


def window_attend_back(pair, shard, qkv, grad, tables, back, select, spread):
    spec = pltpu.PrefetchScalarGridSpec(
        num_scalar_prefetch=1,
        grid=(5,),
        in_specs=[
            pl.BlockSpec((2, 28, SIDE, 960), lambda w, s: (pair, 0, w, 0)),
            pl.BlockSpec((16, SIDE, 640), lambda w, s: (0, w, pair)),
            pl.BlockSpec((256, 384), lambda w, s: (0, 0)),
            pl.BlockSpec((256, 384), lambda w, s: (0, 0)),
            pl.BlockSpec((GROUP, KEYS, 256), lambda w, s: (0, 0, 0)),
            pl.BlockSpec((GROUP, KEYS, 128), lambda w, s: (0, 0, 0)),
        ],
        out_specs=[
            pl.BlockSpec((28, SIDE, 960), lambda w, s: (0, w, 0)),
            pl.BlockSpec((28, SIDE, 960), lambda w, s: (0, w, 0)),
            pl.BlockSpec((256, 384), lambda w, s: (0, 0)),
        ],
        scratch_shapes=[
            pltpu.VMEM((16 * SIDE, 384), jnp.float32),
            pltpu.VMEM((2 * KEYS, 384), jnp.float32),
            pltpu.VMEM((2 * KEYS, 384), jnp.float32),
        ],
    )
    return pl.pallas_call(
        backward_kernel,
        grid_spec=spec,
        out_shape=[
            jax.ShapeDtypeStruct((28, 5 * SIDE, 960), jnp.bfloat16),
            jax.ShapeDtypeStruct((28, 5 * SIDE, 960), jnp.bfloat16),
            jax.ShapeDtypeStruct((256, 384), jnp.float32),
        ],
        compiler_params=pltpu.CompilerParams(vmem_limit_bytes=48 << 20),
        cost_estimate=pl.CostEstimate(flops=60_000_000_000, bytes_accessed=20_000_000, transcendentals=0),
        name="attend_back",
    )(shard, qkv, grad, tables, back, select, spread)


def project_kernel(shard_ref, x_ref, w_ref, bias_ref, out_ref, proj_ref):
    weights = w_ref[0][:, :960]
    for start in range(0, x_ref.shape[0], 448):
        rows = slice(start, start + 448)
        out_ref[0, rows, :] = (dot(x_ref[rows, :], weights, NN) + bias_ref[0]).astype(jnp.bfloat16)
    odd = pl.program_id(0) % 2

    @pl.when(odd == 0)
    def _():
        proj_ref[:, 0:384] = shift_lanes(w_ref[0, :, 896:1280], -64).astype(jnp.bfloat16)

    @pl.when(odd == 1)
    def _():
        lane = lane_iota((1, 128))
        left = (lane < 64).astype(jnp.float32).astype(jnp.bfloat16)
        right = (lane >= 64).astype(jnp.float32).astype(jnp.bfloat16)
        proj_ref[:, 256:384] = proj_ref[:, 256:384] * left + w_ref[0, :, 896:1024] * right
        proj_ref[:, 384:640] = w_ref[0, :, 1024:1280]


def project(shard, x, weights, bias):
    tokens, width = x.shape
    spec = pltpu.PrefetchScalarGridSpec(
        num_scalar_prefetch=1,
        grid=(4,),
        in_specs=[
            pl.BlockSpec((tokens, width), lambda p, s: (0, 0)),
            pl.BlockSpec((1, width, 1280), lambda p, s: (p ^ s[0], 0, 0)),
            pl.BlockSpec((1, 1, 960), lambda p, s: (p ^ s[0], 0, 0)),
        ],
        out_specs=[
            pl.BlockSpec((1, tokens, 960), lambda p, s: (p, 0, 0)),
            pl.BlockSpec((width, 640), lambda p, s: (0, p // 2)),
        ],
    )
    return pl.pallas_call(
        project_kernel,
        grid_spec=spec,
        out_shape=[
            jax.ShapeDtypeStruct((4, tokens, 960), jnp.bfloat16),
            jax.ShapeDtypeStruct((width, 1280), jnp.bfloat16),
        ],
        compiler_params=pltpu.CompilerParams(vmem_limit_bytes=48 << 20),
        cost_estimate=pl.CostEstimate(flops=24_000_000_000, bytes_accessed=35_000_000, transcendentals=0),
        name="project",
    )(shard, x, weights, bias)


def frame_kernel(shard_ref, near_own, near_other, far_own, far_other, w_ref, fold_ref, out_ref, sums_ref):
    total = None
    for p, back_ref in enumerate((near_own, near_other, far_own, far_other)):
        back = back_ref[...]
        piece = dot(back, w_ref[p ^ shard_ref[0]][:, :960], NT)
        total = piece if total is None else total + piece
        column = jnp.sum(back.astype(jnp.float32), axis=0, keepdims=True)

        @pl.when(pl.program_id(0) == 0)
        def _():
            sums_ref[p] = column

        @pl.when(pl.program_id(0) > 0)
        def _():
            sums_ref[p] += column
    total = total.astype(jnp.bfloat16)
    for row in range(out_ref.shape[0]):
        piece = total[row * 80:(row + 1) * 80, :]
        out_ref[row] = dot(fold_ref[...], piece, NN).astype(jnp.bfloat16)


def frame_back(shard, backs, weights, fold):
    width = weights.shape[1]
    chunk = 7
    back_spec = pl.BlockSpec((chunk * 80, 960), lambda g, s: (g, 0))
    spec = pltpu.PrefetchScalarGridSpec(
        num_scalar_prefetch=1,
        grid=(28 // chunk,),
        in_specs=[back_spec] * 4 + [
            pl.BlockSpec((4, width, 1280), lambda g, s: (0, 0, 0), pipeline_mode=pl.Buffered(1)),
            pl.BlockSpec(fold.shape, lambda g, s: (0, 0)),
        ],
        out_specs=[
            pl.BlockSpec((chunk, 64, width), lambda g, s: (g, 0, 0)),
            pl.BlockSpec((4, 1, 960), lambda g, s: (0, 0, 0)),
        ],
    )
    return pl.pallas_call(
        frame_kernel,
        grid_spec=spec,
        out_shape=[
            jax.ShapeDtypeStruct((28, 64, width), jnp.bfloat16),
            jax.ShapeDtypeStruct((4, 1, 960), jnp.float32),
        ],
        compiler_params=pltpu.CompilerParams(vmem_limit_bytes=58 << 20),
        cost_estimate=pl.CostEstimate(flops=1_000_000, bytes_accessed=1_000_000, transcendentals=0),
        name="frame_back",
    )(shard, *backs, weights, fold)


def turn_kernel(x_ref, out_ref):
    out_ref[...] = x_ref[...].T


def turn(x):
    return pl.pallas_call(
        turn_kernel,
        out_shape=jax.ShapeDtypeStruct(x.shape[::-1], x.dtype),
        compiler_params=pltpu.CompilerParams(vmem_limit_bytes=48 << 20),
        cost_estimate=pl.CostEstimate(flops=0, bytes_accessed=12_000_000, transcendentals=0),
        name="turn",
    )(x)


ROWS = 16
FRAME = 28
EARLY, LATE = 6, 12
EPSILON = 1e-06


def swap(values, shifts):
    return lax.ppermute(values, "tensor", shifts)


def own(values, index, axis=0):
    return lax.dynamic_index_in_dim(values, index, axis, keepdims=False)


def gather_small(values, shard):
    parts = [values]
    for step in (1, 2, 3):
        parts.append(swap(values, [(i, (i + step) % 4) for i in range(4)]))
    stack = jnp.stack(parts)
    return jnp.stack([own(stack, (shard - i) % 4) for i in range(4)])


CORES = [(0, 1), (1, 0), (2, 3), (3, 2)]
SIDES = [(0, 2), (2, 0), (1, 3), (3, 1)]


def add_low(left, right):
    return (left.astype(jnp.float32) + right.astype(jnp.float32)).astype(jnp.bfloat16)


def scatter_dp(quarter):
    return lax.psum_scatter(quarter, "dp", scatter_dimension=0, tiled=True)


def after(first, *values):
    return lax.optimization_barrier((first,) + values)[1:]


def sum_everywhere(values):
    values = values + swap(values, CORES)
    values = values + swap(values, SIDES)
    count = lax.axis_size("dp")
    step = 1
    while step < count:
        values = values + lax.ppermute(values, "dp", [(i, i ^ step) for i in range(count)])
        step *= 2
    return values


def statistics(values):
    average = jnp.mean(values, axis=-1, keepdims=True)
    centred = values - average
    rstd = lax.rsqrt(jnp.mean(centred * centred, axis=-1, keepdims=True) + EPSILON)
    return centred * rstd, rstd


def norm_back(grad, gain, hat, rstd):
    scaled = grad * gain
    mean_one = jnp.mean(scaled, axis=-1, keepdims=True)
    mean_two = jnp.mean(scaled * hat, axis=-1, keepdims=True)
    return rstd * (scaled - mean_one - hat * mean_two)


def column_selector():
    column = np.arange(GRID)
    place = SIDE * (column // WIN) + column % WIN
    select = np.zeros((NWIN * SIDE, GRID), np.float32)
    select[place, column] = 1.0
    return jnp.asarray(select, jnp.bfloat16)


def fast_shards(
    inputs,
    cotangent,
    teacher,
    qkv_weight,
    proj_weight,
    up_weight,
    down_weight,
    qv_bias,
    up_bias,
    norm_gains,
    norm_shifts,
    out_biases,
    rel_tables,
):
    f32, bf16 = jnp.float32, jnp.bfloat16
    shard = lax.axis_index("tensor")
    both = ("tensor", "dp")
    tokens = ROWS * GRID
    inner = qkv_weight.shape[1]
    joint = jnp.concatenate([qkv_weight.transpose(1, 0, 2).reshape(inner, 960), proj_weight.T], axis=1)
    joint = jnp.concatenate([joint, up_weight], axis=1)
    joint_all = lax.all_gather(joint, both, axis=0, tiled=True).reshape(4, D, 2560)
    biases = gather_small(jnp.concatenate([qv_bias.reshape(-1), up_bias]), shard)
    qkv_bias = jnp.concatenate(
        [biases[:, :320], jnp.zeros((4, 320), bf16), biases[:, 320:640]], axis=1
    ).astype(f32)
    up_bias_all = biases[:, 640:].astype(f32)

    gains = norm_gains.astype(f32)
    shifts = norm_shifts.astype(f32)
    image = inputs[0]
    above = swap(image[ROWS - EARLY:], [(i, i + 1) for i in range(3)])
    below = swap(image[:LATE], [(i + 1, i) for i in range(3)])
    framed = lax.dynamic_slice_in_dim(
        jnp.concatenate([above, image, below]), EARLY - 2 * shard, FRAME, 0
    )
    frame_hat, _ = statistics(framed.astype(f32))
    inside = (WIN * shard + jnp.arange(FRAME) < GRID)[:, None, None]
    normed = jnp.where(inside, frame_hat * gains[0] + shifts[0], 0.0).astype(bf16)
    select = column_selector()
    windows = jnp.einsum("pc,rcd->rpd", select, normed, preferred_element_type=f32).astype(bf16)
    flat = windows.reshape(FRAME * NWIN * SIDE, D)
    where = shard[None].astype(jnp.int32)
    qkv, proj_full = project(where, flat, joint_all, qkv_bias[:, None, :])
    qkv = qkv.reshape(4, FRAME, NWIN * SIDE, 960)
    tables, back_tables = bias_tables(rel_tables)
    select_keys, spread_keys = selectors()
    flat_turned = turn(flat)
    (down_shard,) = after((joint_all, flat_turned), down_weight.T)
    down_all = lax.all_gather(down_shard, both, axis=0, tiled=True).reshape(4, D, 1280)
    up_all = joint_all[:, :, 1280:]
    attended = window_attend(where, qkv, tables, select_keys)
    attended = jnp.einsum("pc,rpd->rcd", select, attended, preferred_element_type=f32)
    attended = attended.astype(bf16).reshape(tokens, D)

    source = image.astype(f32).reshape(tokens, D)
    branch = jnp.einsum("nk,ck->nc", attended, proj_full, preferred_element_type=f32)
    middle = source + branch + out_biases[0].astype(f32)
    second_hat, second_rstd = statistics(middle)
    normed_two = (second_hat * gains[1] + shifts[1]).astype(bf16)
    hidden = jnp.einsum("nd,tdm->tnm", normed_two, up_all, preferred_element_type=f32)
    hidden = hidden + up_bias_all[:, None, :]
    cdf = 0.5 + 0.5 * lax.erf(hidden * (0.5 ** 0.5))
    active = (hidden * cdf).astype(bf16)
    slope = (cdf + hidden * (jnp.exp(-0.5 * hidden * hidden) * (0.5 / np.pi) ** 0.5)).astype(bf16)
    result = jnp.einsum("tnm,tcm->nc", active, down_all, preferred_element_type=f32)
    result = middle + result + out_biases[1].astype(f32)
    mismatch = result - teacher[0].astype(f32).reshape(tokens, D)
    loss_total = jnp.sum(mismatch * mismatch)
    output = result.astype(bf16)

    result_grad = cotangent[0].astype(f32).reshape(tokens, D) + mismatch
    result_low = result_grad.astype(bf16)
    def down_block(p):
        return jnp.einsum("nc,nm->cm", result_low, own(active, shard ^ p), preferred_element_type=f32)

    sends = [down_block(3).astype(bf16), down_block(1).astype(bf16)]
    down_three, down_one = swap(sends[0], CORES), swap(sends[1], CORES)
    (result_next,) = after(tuple(sends), result_low)
    active_grad = jnp.einsum("nc,tcm->tnm", result_next, down_all, preferred_element_type=f32)
    hidden_grad = active_grad * slope.astype(f32)
    up_bias_acc = jnp.sum(hidden_grad, axis=1)
    hidden_low = hidden_grad.astype(bf16)
    down_far = (down_block(2) + down_three.astype(f32)).astype(bf16)
    down_near = (down_block(0) + down_one.astype(f32)).astype(bf16)
    down_side = swap(down_far, SIDES)
    hidden_low, normed_two = after((down_far, down_near), hidden_low, normed_two)

    def up_block(p):
        return jnp.einsum("nd,nm->dm", normed_two, own(hidden_low, shard ^ p), preferred_element_type=f32)

    sends = [up_block(3).astype(bf16), up_block(1).astype(bf16)]
    up_three, up_one = swap(sends[0], CORES), swap(sends[1], CORES)
    (hidden_next,) = after(tuple(sends), hidden_low)
    second_grad = jnp.einsum("tnm,tdm->nd", hidden_next, up_all, preferred_element_type=f32)
    middle_grad = result_grad + norm_back(second_grad, gains[1], second_hat, second_rstd)
    second_gain = jnp.sum(second_grad * second_hat, axis=0)
    second_shift = jnp.sum(second_grad, axis=0)
    middle_low = middle_grad.astype(bf16)
    attended_grad = jnp.einsum("nc,ck->nk", middle_low, proj_full, preferred_element_type=f32)
    attended_grad = attended_grad.astype(bf16).reshape(ROWS, GRID, D)
    attended_grad = jnp.einsum("pc,rcd->rpd", select, attended_grad, preferred_element_type=f32)
    attended_grad = attended_grad.astype(bf16)
    up_far = (up_block(2) + up_three.astype(f32)).astype(bf16)
    up_near = (up_block(0) + up_one.astype(f32)).astype(bf16)
    up_side = swap(up_far, SIDES)

    def proj_block(p):
        part = attended[:, 320 * p:320 * p + 320]
        return jnp.einsum("nc,nk->ck", middle_low, part, preferred_element_type=f32)

    proj_sends = (proj_block(3).astype(bf16), proj_block(1).astype(bf16))
    proj_three, proj_one = swap(proj_sends[0], CORES), swap(proj_sends[1], CORES)
    (down_near,) = after((up_far, up_near, proj_sends), down_near)
    down_quarter = add_low(down_near, down_side)
    (grad_far,) = after((up_far, up_near, down_quarter), attended_grad)
    far_own, far_other, far_sums = window_attend_back(
        1, where, qkv, grad_far, tables, back_tables, select_keys, spread_keys
    )

    def flatten(back):
        return back.reshape(FRAME * NWIN * SIDE, 960)

    def qkv_block(tokens_in, back):
        return jnp.einsum("dn,nc->dc", tokens_in, back, preferred_element_type=f32)

    far_own, far_other = flatten(far_own), flatten(far_other)
    qkv_send = qkv_block(flat_turned, far_other).astype(bf16)
    qkv_three = swap(qkv_send, CORES)
    flat_far, up_side, down_grad, _ = lax.optimization_barrier(
        (flat_turned, up_side, scatter_dp(down_quarter), qkv_send)
    )
    up_quarter = add_low(up_near, up_side)
    proj_far = (proj_block(2) + proj_three.astype(f32)).astype(bf16)
    proj_near = (proj_block(0) + proj_one.astype(f32)).astype(bf16)
    qkv_far = (qkv_block(flat_far, far_own) + qkv_three.astype(f32)).astype(bf16)
    joint_far = jnp.concatenate([qkv_far, proj_far], axis=1)
    joint_far, proj_near, up_quarter, grad_near = lax.optimization_barrier(
        (joint_far, proj_near, up_quarter, attended_grad)
    )
    far_side = swap(joint_far, SIDES)
    near_own, near_other, near_sums = window_attend_back(
        0, where, qkv, grad_near, tables, back_tables, select_keys, spread_keys
    )
    near_own, near_other = flatten(near_own), flatten(near_other)
    qkv_send = qkv_block(flat_turned, near_other).astype(bf16)
    qkv_one = swap(qkv_send, CORES)
    backs = after(qkv_send, near_own, near_other, far_own, far_other)
    frame_grad, bias_sums = frame_back(where, backs, joint_all, select.T)
    spread = jnp.zeros((EARLY + ROWS + LATE, GRID, D), bf16)
    spread = lax.dynamic_update_slice_in_dim(spread, frame_grad, EARLY - 2 * shard, 0)
    flat_near, far_side, spread = lax.optimization_barrier((flat_turned, far_side, spread))
    qkv_near = qkv_block(flat_near, near_own) + qkv_one.astype(f32)
    near = jnp.concatenate([qkv_near.astype(bf16), proj_near], axis=1)
    joint_quarter = add_low(near, far_side)
    up_grad, joint_quarter = lax.optimization_barrier((scatter_dp(up_quarter), joint_quarter))
    joint_grad = scatter_dp(joint_quarter)
    table_sums = far_sums + near_sums
    bias_sums = bias_sums[:, 0]
    qv_acc = jnp.stack([bias_sums[:, :320], bias_sums[:, 640:]], axis=1)
    qv_acc = jnp.stack([own(qv_acc, shard ^ t) for t in range(4)])
    table_sums = table_sums[:, :320].reshape(2, GROUP, 32, GROUP, HEAD_DIM)
    table_acc = jnp.einsum("phrhd->prd", table_sums)
    table_acc = jnp.stack([table_acc[0, :27][::-1], table_acc[1, :27]])
    from_next = swap(spread[:EARLY], [(i + 1, i) for i in range(3)])
    from_before = swap(spread[EARLY + ROWS:], [(i, i + 1) for i in range(3)])
    first_grad = spread[EARLY:EARLY + ROWS].astype(f32)
    first_grad = first_grad + jnp.pad(from_next.astype(f32), ((ROWS - EARLY, 0), (0, 0), (0, 0)))
    first_grad = first_grad + jnp.pad(from_before.astype(f32), ((0, ROWS - LATE), (0, 0), (0, 0)))
    first_grad = first_grad.reshape(tokens, D)
    first_hat, first_rstd = statistics(source)
    first_gain = jnp.sum(first_grad * first_hat, axis=0)
    first_shift = jnp.sum(first_grad, axis=0)
    input_grad = middle_grad + norm_back(first_grad, gains[0], first_hat, first_rstd)

    small = [
        qv_acc, up_bias_acc, first_gain, second_gain, first_shift, second_shift,
        jnp.sum(middle_grad, axis=0), jnp.sum(result_grad, axis=0), table_acc, loss_total,
    ]
    sums = sum_everywhere(jnp.concatenate([part.reshape(-1) for part in small]))
    parts = []
    place = 0
    for part in small:
        parts.append(sums[place:place + part.size].reshape(part.shape))
        place += part.size
    qv_sum, up_sum, gain_one, gain_two, shift_one, shift_two, bias_one, bias_two, table_grad, loss_sum = parts
    loss = loss_sum / (tokens * D * lax.axis_size("dp") * lax.axis_size("tensor"))
    return (
        output.reshape(1, ROWS, GRID, D),
        input_grad.reshape(1, ROWS, GRID, D),
        loss,
        joint_grad[:, :960].reshape(inner, 3, 320).transpose(1, 0, 2).astype(f32),
        joint_grad[:, 960:].T.astype(f32),
        up_grad.astype(f32),
        down_grad.T.astype(f32),
        own(qv_sum, shard),
        own(up_sum, shard),
        jnp.stack([gain_one, gain_two]),
        jnp.stack([shift_one, shift_two]),
        jnp.stack([bias_one, bias_two]),
        table_grad,
    )


def solution(mesh):
    in_specs = (
        P("dp", "tensor", None, None),
        P("dp", "tensor", None, None),
        P("dp", "tensor", None, None),
        P(None, "dp", "tensor"),
        P("tensor", "dp"),
        P("dp", "tensor"),
        P("tensor", "dp"),
        P(None, "tensor"),
        P("tensor"),
        P(),
        P(),
        P(),
        P(),
    )
    out_specs = (
        P("dp", "tensor", None, None),
        P("dp", "tensor", None, None),
        P(),
        P(None, "dp", "tensor"),
        P("tensor", "dp"),
        P("dp", "tensor"),
        P("tensor", "dp"),
        P(None, "tensor"),
        P("tensor"),
        P(),
        P(),
        P(),
        P(),
    )
    fits = mesh.shape["tensor"] == 4 and GRID // mesh.shape["tensor"] == 16
    shards = fast_shards if fits else general_shards
    return jax.shard_map(shards, mesh=mesh, in_specs=in_specs, out_specs=out_specs, check_vma=False)
```

```python
from functools import partial

import jax
import jax.numpy as jnp
import numpy as np
from jax import lax
from jax.experimental import pallas as pl
from jax.experimental.pallas import tpu as pltpu
from jax.sharding import PartitionSpec as P

D = 1280
HEAD_DIM = 80
GRID = 64
WIN = 14
PGRID = 70
NWIN = 5


highest = lax.Precision.HIGHEST


def layer_norm(values, gain_vector, shift_vector):
    average = jnp.mean(values, axis=-1, keepdims=True)
    centred = values - average
    variance = jnp.mean(centred * centred, axis=-1, keepdims=True)
    return centred * lax.rsqrt(variance + 1e-06) * gain_vector + shift_vector


def exact_gelu(values):
    return jax.nn.gelu(values, approximate=False)


def offset_tables(window):
    position = jnp.arange(window * window)
    across = jnp.arange(window)
    ranks = jnp.arange(2 * window - 1)
    high_sel = (
        position[:, None, None] // window - across[None, :, None] + window - 1
        == ranks[None, None, :]
    ).astype(jnp.float32)
    wide_sel = (
        position[:, None, None] % window - across[None, :, None] + window - 1
        == ranks[None, None, :]
    ).astype(jnp.float32)
    return (high_sel, wide_sel)


def to_windows(grid_values):
    extra = PGRID - GRID
    padded = jnp.pad(grid_values, ((0, extra), (0, extra), (0, 0)))
    channels = grid_values.shape[-1]
    shaped = padded.reshape(NWIN, WIN, NWIN, WIN, channels).transpose(0, 2, 1, 3, 4)
    return shaped.reshape(NWIN, NWIN, WIN * WIN, channels)


def from_windows(windowed):
    channels = windowed.shape[-1]
    shaped = windowed.reshape(NWIN, NWIN, WIN, WIN, channels).transpose(0, 2, 1, 3, 4)
    return shaped.reshape(PGRID, PGRID, channels)[:GRID, :GRID]


def score_block(queries, key_rows, tables, selectors):
    table_high, table_wide = tables
    high_sel, wide_sel = selectors
    raw = jnp.einsum(
        "wqhc,wkhc->whqk", queries, key_rows, preferred_element_type=jnp.float32
    ) * HEAD_DIM ** (-0.5)
    along_high = jnp.einsum(
        "wqhc,rc->wqhr", queries, table_high, preferred_element_type=jnp.float32
    )
    along_wide = jnp.einsum(
        "wqhc,rc->wqhr", queries, table_wide, preferred_element_type=jnp.float32
    )
    bias_high = jnp.einsum("wqhr,qkr->whqk", along_high, high_sel, precision=highest)
    bias_wide = jnp.einsum("wqhr,qkr->whqk", along_wide, wide_sel, precision=highest)
    shaped = (
        raw.reshape(raw.shape[:3] + (WIN, WIN)) + bias_high[..., :, None] + bias_wide[..., None, :]
    )
    return shaped.reshape(raw.shape)


def attend_row(block_parts, tables, selectors):
    queries, key_rows, value_rows = block_parts
    scores = score_block(queries, key_rows, tables, selectors)
    row_max = jnp.max(scores, axis=-1, keepdims=True)
    shifted = jnp.exp(scores - row_max)
    row_total = jnp.sum(shifted, axis=-1, keepdims=True)
    probs_low = (shifted / row_total).astype(jnp.bfloat16)
    attended = jnp.einsum(
        "whqk,wkhc->wqhc", probs_low, value_rows, preferred_element_type=jnp.float32
    )
    return (attended.astype(jnp.bfloat16), (row_max + jnp.log(row_total))[..., 0])


def attend_back(block_parts, tables, selectors):
    queries, key_rows, value_rows, attended_grad, log_total = block_parts
    high_sel, wide_sel = selectors
    scores = score_block(queries, key_rows, tables, selectors)
    probs = jnp.exp(scores - log_total[..., None])
    probs_grad = jnp.einsum(
        "wqhc,wkhc->whqk", attended_grad, value_rows, preferred_element_type=jnp.float32
    )
    value_grad = jnp.einsum(
        "whqk,wqhc->wkhc",
        probs.astype(jnp.bfloat16),
        attended_grad,
        preferred_element_type=jnp.float32,
    )
    scores_grad = probs * (probs_grad - jnp.sum(probs * probs_grad, axis=-1, keepdims=True))
    scores_low = scores_grad.astype(jnp.bfloat16)
    query_grad = jnp.einsum(
        "whqk,wkhc->wqhc", scores_low, key_rows, preferred_element_type=jnp.float32
    ) * HEAD_DIM ** (-0.5)
    key_grad = jnp.einsum(
        "whqk,wqhc->wkhc", scores_low, queries, preferred_element_type=jnp.float32
    ) * HEAD_DIM ** (-0.5)
    shaped = scores_grad.reshape(scores_grad.shape[:3] + (WIN, WIN))
    rank_high = jnp.einsum("whqa,qar->wqhr", jnp.sum(shaped, axis=-1), high_sel, precision=highest)
    rank_wide = jnp.einsum("whqb,qbr->wqhr", jnp.sum(shaped, axis=-2), wide_sel, precision=highest)
    table_high = tables[0].astype(jnp.float32)
    table_wide = tables[1].astype(jnp.float32)
    query_grad = query_grad + jnp.einsum("wqhr,rc->wqhc", rank_high, table_high, precision=highest)
    query_grad = query_grad + jnp.einsum("wqhr,rc->wqhc", rank_wide, table_wide, precision=highest)
    query_wide = queries.astype(jnp.float32)
    table_grad = jnp.stack(
        [
            jnp.einsum("wqhr,wqhc->rc", rank_high, query_wide, precision=highest),
            jnp.einsum("wqhr,wqhc->rc", rank_wide, query_wide, precision=highest),
        ]
    )
    return (query_grad, key_grad, value_grad, table_grad)


def general_shards(
    inputs,
    cotangent,
    teacher,
    qkv_weight,
    proj_weight,
    up_weight,
    down_weight,
    qv_bias,
    up_bias,
    norm_gains,
    norm_shifts,
    out_biases,
    rel_tables,
):
    qkv_full, proj_full, up_full, down_full = (
        lax.all_gather(qkv_weight, "dp", axis=1, tiled=True),
        lax.all_gather(proj_weight, "dp", axis=1, tiled=True),
        lax.all_gather(up_weight, "dp", axis=0, tiled=True),
        lax.all_gather(down_weight, "dp", axis=1, tiled=True),
    )
    up_matrix, down_matrix, up_bias_all = (up_full, down_full, up_bias)
    images, row_count = (inputs.shape[0], inputs.shape[1])
    local_width = qkv_full.shape[2]
    head_count = local_width // HEAD_DIM
    head_shape = (NWIN, NWIN, WIN * WIN, head_count, HEAD_DIM)
    selectors = offset_tables(WIN)
    tables = (rel_tables[0], rel_tables[1])
    gains_wide = norm_gains.astype(jnp.float32)
    shifts_wide = norm_shifts.astype(jnp.float32)
    source = inputs[0].astype(jnp.float32)
    normed = layer_norm(source, gains_wide[0], shifts_wide[0]).astype(jnp.bfloat16)
    gathered = lax.all_gather(normed, "tensor", axis=0, tiled=True)
    windows = to_windows(gathered)
    projected = jnp.einsum("abpd,sdc->sabpc", windows, qkv_full, preferred_element_type=jnp.float32)
    queries = (projected[0] + qv_bias[0]).astype(jnp.bfloat16).reshape(head_shape)
    key_rows = projected[1].astype(jnp.bfloat16).reshape(head_shape)
    value_rows = (projected[2] + qv_bias[1]).astype(jnp.bfloat16).reshape(head_shape)
    attended, log_totals = lax.map(
        partial(attend_row, tables=tables, selectors=selectors), (queries, key_rows, value_rows)
    )
    grid_out = from_windows(attended.reshape(NWIN, NWIN, WIN * WIN, local_width))
    row_piece = grid_out
    attn_branch = lax.psum_scatter(
        jnp.einsum("xyc,cd->xyd", row_piece, proj_full, preferred_element_type=jnp.float32).astype(
            jnp.bfloat16
        ),
        "tensor",
        scatter_dimension=0,
        tiled=True,
    ).astype(jnp.float32)
    middle = source + attn_branch + out_biases[0].astype(jnp.float32)
    normed_two = layer_norm(middle, gains_wide[1], shifts_wide[1]).astype(jnp.bfloat16)
    mlp_input = lax.all_gather(normed_two, "tensor", axis=0, tiled=True)
    hidden = (
        jnp.einsum("xyd,dm->xym", mlp_input, up_matrix, preferred_element_type=jnp.float32)
        + up_bias_all
    )
    active = exact_gelu(hidden).astype(jnp.bfloat16)
    row_piece = active
    mlp_branch = lax.psum_scatter(
        jnp.einsum(
            "xym,md->xyd", row_piece, down_matrix, preferred_element_type=jnp.float32
        ).astype(jnp.bfloat16),
        "tensor",
        scatter_dimension=0,
        tiled=True,
    ).astype(jnp.float32)
    result = middle + mlp_branch + out_biases[1].astype(jnp.float32)
    mismatch = result - teacher[0].astype(jnp.float32)
    loss_total = jnp.sum(mismatch * mismatch)
    outputs = [result.astype(jnp.bfloat16)]
    result_grad = cotangent[0].astype(jnp.float32) + mismatch
    result_low = result_grad.astype(jnp.bfloat16)
    grad_rows = lax.all_gather(result_low, "tensor", axis=0, tiled=True)
    down_acc = jnp.einsum("xym,xyd->md", active, grad_rows, preferred_element_type=jnp.float32)
    active_grad = jnp.einsum(
        "xyd,md->xym", grad_rows, down_matrix, preferred_element_type=jnp.float32
    )
    gelu_value, gelu_back = jax.vjp(exact_gelu, hidden)
    hidden_grad = gelu_back(active_grad)[0]
    up_bias_acc = jnp.sum(hidden_grad, axis=(0, 1))
    hidden_low = hidden_grad.astype(jnp.bfloat16)
    up_acc = jnp.einsum("xyd,xym->dm", mlp_input, hidden_low, preferred_element_type=jnp.float32)
    row_piece = hidden_low
    second_grad = lax.psum_scatter(
        jnp.einsum("xym,dm->xyd", row_piece, up_matrix, preferred_element_type=jnp.float32).astype(
            jnp.bfloat16
        ),
        "tensor",
        scatter_dimension=0,
        tiled=True,
    ).astype(jnp.float32)
    second_value, second_back = jax.vjp(layer_norm, middle, gains_wide[1], shifts_wide[1])
    middle_part, second_gain, second_shift = second_back(second_grad)
    middle_grad = result_grad + middle_part
    out_bias_acc = jnp.stack([jnp.sum(middle_grad, axis=(0, 1)), jnp.sum(result_grad, axis=(0, 1))])
    middle_low = middle_grad.astype(jnp.bfloat16)
    gathered_grad = lax.all_gather(middle_low, "tensor", axis=0, tiled=True)
    proj_acc = jnp.einsum(
        "xyc,xyd->cd", grid_out, gathered_grad, preferred_element_type=jnp.float32
    )
    attended_grad = jnp.einsum(
        "xyd,cd->xyc", gathered_grad, proj_full, preferred_element_type=jnp.float32
    ).astype(jnp.bfloat16)
    grad_windows = to_windows(attended_grad).reshape(head_shape)
    query_grad, key_grad, value_grad, table_parts = lax.map(
        partial(attend_back, tables=tables, selectors=selectors),
        (queries, key_rows, value_rows, grad_windows, log_totals),
    )
    table_acc = jnp.sum(table_parts, axis=0)
    query_flat = query_grad.reshape(NWIN, NWIN, WIN * WIN, local_width)
    key_flat = key_grad.reshape(NWIN, NWIN, WIN * WIN, local_width)
    value_flat = value_grad.reshape(NWIN, NWIN, WIN * WIN, local_width)
    qv_acc = jnp.stack([jnp.sum(query_flat, axis=(0, 1, 2)), jnp.sum(value_flat, axis=(0, 1, 2))])
    stacked = jnp.stack([query_flat, key_flat, value_flat]).astype(jnp.bfloat16)
    qkv_acc = jnp.einsum("abpd,sabpc->sdc", windows, stacked, preferred_element_type=jnp.float32)
    normed_back = jnp.einsum(
        "sabpc,sdc->abpd", stacked, qkv_full, preferred_element_type=jnp.float32
    )
    first_grad = lax.psum_scatter(
        from_windows(normed_back).astype(jnp.bfloat16), "tensor", scatter_dimension=0, tiled=True
    ).astype(jnp.float32)
    first_value, first_back = jax.vjp(layer_norm, source, gains_wide[0], shifts_wide[0])
    source_part, first_gain, first_shift = first_back(first_grad)
    gain_acc = jnp.stack([first_gain, second_gain])
    shift_acc = jnp.stack([first_shift, second_shift])
    input_grads = [middle_grad + source_part]
    qkv_grad, proj_grad, up_grad, down_grad = (
        lax.psum_scatter(
            qkv_acc.astype(jnp.bfloat16), "dp", scatter_dimension=1, tiled=True
        ).astype(jnp.float32),
        lax.psum_scatter(
            proj_acc.astype(jnp.bfloat16), "dp", scatter_dimension=1, tiled=True
        ).astype(jnp.float32),
        lax.psum_scatter(up_acc.astype(jnp.bfloat16), "dp", scatter_dimension=0, tiled=True).astype(
            jnp.float32
        ),
        lax.psum_scatter(
            down_acc.astype(jnp.bfloat16), "dp", scatter_dimension=1, tiled=True
        ).astype(jnp.float32),
    )
    qv_grad, up_bias_grad = lax.psum((qv_acc, up_bias_acc), "dp")
    gains_grad, shifts_grad, out_grad, table_grad, loss_sum = lax.psum(
        (gain_acc, shift_acc, out_bias_acc, table_acc, loss_total), ("dp", "tensor")
    )
    element_count = images * row_count * GRID * D * lax.axis_size("dp") * lax.axis_size("tensor")
    loss = loss_sum / element_count
    return (
        jnp.stack(outputs),
        jnp.stack(input_grads),
        loss,
        qkv_grad,
        proj_grad,
        up_grad,
        down_grad,
        qv_grad,
        up_bias_grad,
        gains_grad,
        shifts_grad,
        out_grad,
        table_grad,
    )


SIDE = 16
GROUP = 4
KEYS = WIN * SIDE
SLABS = ((0, 128), (0, 256), (128, 256), (128, 384))
SCALE = HEAD_DIM ** (-0.5)
LOG2E = 1.4426950408889634
NT = (((1,), (1,)), ((), ()))
TN = (((0,), (0,)), ((), ()))
NN = (((1,), (0,)), ((), ()))


def dot(a, b, dims):
    return lax.dot_general(a, b, dims, preferred_element_type=jnp.float32)


def bias_tables(rel_tables):
    tables = rel_tables.astype(jnp.bfloat16)

    def place(rows):
        padded = jnp.pad(rows, ((0, 5), (0, 0)))
        eye = jnp.eye(GROUP, dtype=jnp.bfloat16)
        spread = eye[:, None, :, None] * padded[None, :, None, :]
        return spread.reshape(GROUP * 32, GROUP * HEAD_DIM)

    forward = jnp.concatenate([place(tables[0][::-1]), place(tables[1][::-1])])
    backward = jnp.concatenate([place(tables[0][::-1]), place(tables[1])])
    lanes = ((0, 0), (0, 64))
    return jnp.pad(forward, lanes), jnp.pad(backward, lanes)


def selectors():
    key = np.arange(KEYS)
    high, wide = key // SIDE, key % SIDE
    fwd = np.zeros((GROUP, KEYS, 128), np.float32)
    bwd = np.zeros((GROUP, KEYS, 128), np.float32)
    real = wide < WIN
    for head in range(GROUP):
        for j in range(KEYS):
            if real[j]:
                fwd[head, j, 32 * head + high[j]] = 1.0
                fwd[head, j, 32 * head + 16 + wide[j]] = 1.0
                bwd[head, j, 32 * head + high[j]] = 1.0
                bwd[head, j, 32 * head + 16 + 13 - wide[j]] = 1.0
            else:
                fwd[head, j, 32 * head + 14] = -1e30
    fwd = np.concatenate([fwd, fwd], axis=-1)
    return jnp.asarray(fwd, jnp.bfloat16), jnp.asarray(bwd, jnp.bfloat16)


def lane_iota(shape):
    return lax.broadcasted_iota(jnp.int32, shape, 1)


def head_mask(values, head, low):
    lane = lane_iota((1, values.shape[1])) + low
    inside = (lane >= HEAD_DIM * head) & (lane < HEAD_DIM * head + HEAD_DIM)
    return values * inside.astype(jnp.float32).astype(jnp.bfloat16)


def shift_lanes(values, amount):
    wide = values.astype(jnp.float32)
    return pltpu.roll(wide, amount % wide.shape[1], 1)


def load_group(qkv_ref, part, first):
    rows = qkv_ref.shape[1]
    q = qkv_ref[part, pl.ds(first, 16), :, 0:384].reshape(16 * SIDE, 384)
    k = qkv_ref[part, :, :, 256:640].reshape(rows * SIDE, 384)
    k = shift_lanes(k, -64).astype(jnp.bfloat16)
    v = qkv_ref[part, :, :, 640:960].reshape(rows * SIDE, 320)
    return q, k, v


def by_side(values, first):
    row = lax.broadcasted_iota(jnp.int32, (16 * SIDE, 1), 0)
    upper = (row < (WIN - first) * SIDE).astype(jnp.float32)
    return values * upper.astype(jnp.bfloat16), values * (1.0 - upper).astype(jnp.bfloat16)


def bias_rows(q, tables, first):
    along = dot(q, tables, NT) * (HEAD_DIM ** 0.5)
    high, wide = along[:, :128], along[:, 128:]
    pieces = []
    lane = lane_iota((SIDE, 128)) % 32
    for row in range(16):
        ih = lax.rem(first + row, WIN)
        rows = slice(row * SIDE, (row + 1) * SIDE)
        up = pltpu.roll(high[rows], lax.rem(ih + 115, 128), 1)
        across = pltpu.roll(wide[rows], 3, 1, stride=1, stride_axis=0)
        both = jnp.where(lane < 16, up, across)
        pieces.append(jnp.where(lane == 14, 1.0, both))
    both = jnp.concatenate(pieces)
    upper = both.astype(jnp.bfloat16)
    lower = (both - upper.astype(jnp.float32)).astype(jnp.bfloat16)
    return jnp.concatenate([upper, lower], axis=1)


def beside(upper, lower):
    return jnp.concatenate([upper, lower], axis=1)


def score_rows(q_sides, keys, bias, select, head):
    low, high = SLABS[head]
    left = jnp.concatenate([q_sides[0][:, low:high], q_sides[1][:, low:high], bias], axis=1)
    right = jnp.concatenate([keys[:KEYS], keys[KEYS:], select], axis=1)
    return dot(left, right, NT)


def softmax_rows(scores):
    top = jnp.max(scores, axis=1, keepdims=True)
    raised = jnp.exp2((scores - top) * (SCALE * LOG2E))
    total = jnp.sum(raised, axis=1, keepdims=True)
    return raised * (1.0 / total)


def pick_side(both, first):
    width = both.shape[1] // 2
    row = lax.broadcasted_iota(jnp.int32, (16 * SIDE, 1), 0)
    return jnp.where(row < (WIN - first) * SIDE, both[:, :width], both[:, width:])


def pad_lanes(values, width):
    missing = width - values.shape[1]
    if missing == 0:
        return values
    return jnp.concatenate([values, jnp.zeros((values.shape[0], missing), values.dtype)], axis=1)


def forward_kernel(shard_ref, qkv_ref, table_ref, select_ref, out_ref, acc):
    first = 2 * shard_ref[0]
    for part in range(2):
        q, k, v = load_group(qkv_ref, part, first)
        q_sides = by_side(q, first)
        bias = bias_rows(q, table_ref[...], first)
        v = pad_lanes(v, 384)
        scores = []
        for head in range(GROUP):
            low, high = SLABS[head]
            keys = head_mask(k[:, low:high], head, low)
            scores.append(score_rows(q_sides, keys, bias, select_ref[head], head))
        all_probs = [softmax_rows(rows).astype(jnp.bfloat16) for rows in scores]
        for head in range(GROUP):
            low, high = SLABS[head]
            probs = all_probs[head]
            values = head_mask(v[:, low:high], head, low)
            piece = pick_side(dot(probs, beside(values[:KEYS], values[KEYS:]), NN), first)
            if head == 0:
                acc[part, :, 0:128] = piece
                acc[part, :, 128:384] = jnp.zeros((16 * SIDE, 256), jnp.float32)
            else:
                acc[part, :, low:high] += piece
    second = pltpu.roll(acc[1], 64, 1)
    middle = acc[0, :, 256:384] + second[:, 0:128]
    whole = jnp.concatenate([acc[0, :, 0:256], middle, second[:, 128:384]], axis=1)
    out_ref[...] = whole.astype(jnp.bfloat16).reshape(16, SIDE, 640)


def window_attend(shard, qkv, tables, select):
    spec = pltpu.PrefetchScalarGridSpec(
        num_scalar_prefetch=1,
        grid=(5, 2),
        in_specs=[
            pl.BlockSpec((2, 28, SIDE, 960), lambda w, p, s: (p, 0, w, 0)),
            pl.BlockSpec((256, 384), lambda w, p, s: (0, 0)),
            pl.BlockSpec((GROUP, KEYS, 256), lambda w, p, s: (0, 0, 0)),
        ],
        out_specs=pl.BlockSpec((16, SIDE, 640), lambda w, p, s: (0, w, p)),
        scratch_shapes=[pltpu.VMEM((2, 16 * SIDE, 384), jnp.float32)],
    )
    return pl.pallas_call(
        forward_kernel,
        grid_spec=spec,
        out_shape=jax.ShapeDtypeStruct((16, 5 * SIDE, 1280), jnp.bfloat16),
        compiler_params=pltpu.CompilerParams(vmem_limit_bytes=48 << 20),
        cost_estimate=pl.CostEstimate(flops=50_000_000_000, bytes_accessed=20_000_000, transcendentals=0),
        name="attend",
    )(shard, qkv, tables, select)


def backward_kernel(
    shard_ref, qkv_ref, grad_ref, table_ref, back_ref, select_ref, spread_ref, own_ref, other_ref, sums_ref, dq, dk, dv
):
    first = 2 * shard_ref[0]
    queries = 16 * SIDE

    @pl.when(pl.program_id(0) == 0)
    def _():
        sums_ref[...] = jnp.zeros_like(sums_ref)

    lane = lane_iota((SIDE, 128)) % 32
    for part, out_ref in enumerate((own_ref, other_ref)):
        q, k, v = load_group(qkv_ref, part, first)
        v = pad_lanes(v, 384)
        if part == 0:
            go = grad_ref[:, :, 0:384].reshape(queries, 384)
        else:
            go = shift_lanes(grad_ref[:, :, 256:640].reshape(queries, 384), -64).astype(jnp.bfloat16)
        q_sides = by_side(q, first)
        go_sides = by_side(go, first)
        bias = bias_rows(q, table_ref[...], first)
        dq[...] = jnp.zeros_like(dq)
        dk[...] = jnp.zeros_like(dk)
        dv[...] = jnp.zeros_like(dv)
        marks = jnp.zeros((queries, 128), jnp.float32)
        all_keys, scores, grads = [], [], []
        for head in range(GROUP):
            low, high = SLABS[head]
            keys = head_mask(k[:, low:high], head, low)
            values = head_mask(v[:, low:high], head, low)
            all_keys.append(keys)
            scores.append(score_rows(q_sides, keys, bias, select_ref[head], head))
            go_both = beside(go_sides[0][:, low:high], go_sides[1][:, low:high])
            grads.append(dot(go_both, beside(values[:KEYS], values[KEYS:]), NT))
        for head in range(GROUP):
            low, high = SLABS[head]
            keys, probs_grad = all_keys[head], grads[head]
            probs = softmax_rows(scores[head])
            probs_low = probs.astype(jnp.bfloat16)
            weighted = probs * probs_grad
            scores_grad = weighted - probs * jnp.sum(weighted, axis=1, keepdims=True)
            scores_low = scores_grad.astype(jnp.bfloat16)
            width = high - low
            go_head = beside(*(head_mask(side[:, low:high], head, low) for side in go_sides))
            q_head = beside(*(head_mask(side[:, low:high], head, low) for side in q_sides))
            value_grad = dot(probs_low, go_head, TN)
            key_grad = dot(scores_low, q_head, TN)
            for side in range(2):
                span = slice(side * KEYS, (side + 1) * KEYS)
                lanes = slice(side * width, (side + 1) * width)
                dv[span, low:high] += value_grad[:, lanes]
                dk[span, low:high] += key_grad[:, lanes]
            back = jnp.concatenate([keys[:KEYS], keys[KEYS:], spread_ref[head]], axis=1)
            joint = dot(scores_low, back, NN)
            dq[:, low:high] += pick_side(joint[:, :2 * width], first)
            marks = marks + joint[:, 2 * width:]
        highs, wides = [], []
        for row in range(16):
            ih = lax.rem(first + row, WIN)
            piece = marks[row * SIDE:(row + 1) * SIDE]
            highs.append(pltpu.roll(jnp.where(lane < 14, piece, 0.0), 13 - ih, 1))
            across = jnp.where((lane >= 16) & (lane < 30), piece, 0.0)
            wides.append(pltpu.roll(across, 112, 1, stride=1, stride_axis=0))
        ranks = jnp.concatenate([jnp.concatenate(highs), jnp.concatenate(wides)], axis=1).astype(jnp.bfloat16)
        dq_full = (dq[...] * SCALE + dot(ranks, back_ref[...], NN)).reshape(16, SIDE, 384)
        sums_ref[...] += dot(ranks, q, TN)
        dk_all = pltpu.roll(dk[...] * SCALE, 64, 1)
        joint = lane_iota((28 * SIDE, 128))
        middle = jnp.where(joint < 64, 0.0, dk_all[:, 0:128])
        right = jnp.concatenate([middle, dk_all[:, 128:384]], axis=1).reshape(28, SIDE, 384)
        out_ref[:, :, 0:256] = jnp.zeros((28, SIDE, 256), jnp.bfloat16)
        out_ref[:, :, 256:640] = right.astype(jnp.bfloat16)
        own_rows = pl.ds(first, 16)
        out_ref[own_rows, :, 0:256] = dq_full[:, :, 0:256].astype(jnp.bfloat16)
        edge = out_ref[own_rows, :, 256:384].astype(jnp.float32) + dq_full[:, :, 256:384]
        out_ref[own_rows, :, 256:384] = edge.astype(jnp.bfloat16)
        out_ref[:, :, 640:960] = dv[:, 0:320].astype(jnp.bfloat16).reshape(28, SIDE, 320)


def window_attend_back(pair, shard, qkv, grad, tables, back, select, spread):
    spec = pltpu.PrefetchScalarGridSpec(
        num_scalar_prefetch=1,
        grid=(5,),
        in_specs=[
            pl.BlockSpec((2, 28, SIDE, 960), lambda w, s: (pair, 0, w, 0)),
            pl.BlockSpec((16, SIDE, 640), lambda w, s: (0, w, pair)),
            pl.BlockSpec((256, 384), lambda w, s: (0, 0)),
            pl.BlockSpec((256, 384), lambda w, s: (0, 0)),
            pl.BlockSpec((GROUP, KEYS, 256), lambda w, s: (0, 0, 0)),
            pl.BlockSpec((GROUP, KEYS, 128), lambda w, s: (0, 0, 0)),
        ],
        out_specs=[
            pl.BlockSpec((28, SIDE, 960), lambda w, s: (0, w, 0)),
            pl.BlockSpec((28, SIDE, 960), lambda w, s: (0, w, 0)),
            pl.BlockSpec((256, 384), lambda w, s: (0, 0)),
        ],
        scratch_shapes=[
            pltpu.VMEM((16 * SIDE, 384), jnp.float32),
            pltpu.VMEM((2 * KEYS, 384), jnp.float32),
            pltpu.VMEM((2 * KEYS, 384), jnp.float32),
        ],
    )
    return pl.pallas_call(
        backward_kernel,
        grid_spec=spec,
        out_shape=[
            jax.ShapeDtypeStruct((28, 5 * SIDE, 960), jnp.bfloat16),
            jax.ShapeDtypeStruct((28, 5 * SIDE, 960), jnp.bfloat16),
            jax.ShapeDtypeStruct((256, 384), jnp.float32),
        ],
        compiler_params=pltpu.CompilerParams(vmem_limit_bytes=48 << 20),
        cost_estimate=pl.CostEstimate(flops=60_000_000_000, bytes_accessed=20_000_000, transcendentals=0),
        name="attend_back",
    )(shard, qkv, grad, tables, back, select, spread)


def project_kernel(shard_ref, x_ref, w_ref, bias_ref, out_ref, proj_ref):
    weights = w_ref[0][:, :960]
    for start in range(0, x_ref.shape[0], 448):
        rows = slice(start, start + 448)
        out_ref[0, rows, :] = (dot(x_ref[rows, :], weights, NN) + bias_ref[0]).astype(jnp.bfloat16)
    odd = pl.program_id(0) % 2

    @pl.when(odd == 0)
    def _():
        proj_ref[:, 0:384] = shift_lanes(w_ref[0, :, 896:1280], -64).astype(jnp.bfloat16)

    @pl.when(odd == 1)
    def _():
        lane = lane_iota((1, 128))
        left = (lane < 64).astype(jnp.float32).astype(jnp.bfloat16)
        right = (lane >= 64).astype(jnp.float32).astype(jnp.bfloat16)
        proj_ref[:, 256:384] = proj_ref[:, 256:384] * left + w_ref[0, :, 896:1024] * right
        proj_ref[:, 384:640] = w_ref[0, :, 1024:1280]


def project(shard, x, weights, bias):
    tokens, width = x.shape
    spec = pltpu.PrefetchScalarGridSpec(
        num_scalar_prefetch=1,
        grid=(4,),
        in_specs=[
            pl.BlockSpec((tokens, width), lambda p, s: (0, 0)),
            pl.BlockSpec((1, width, 1280), lambda p, s: (p ^ s[0], 0, 0)),
            pl.BlockSpec((1, 1, 960), lambda p, s: (p ^ s[0], 0, 0)),
        ],
        out_specs=[
            pl.BlockSpec((1, tokens, 960), lambda p, s: (p, 0, 0)),
            pl.BlockSpec((width, 640), lambda p, s: (0, p // 2)),
        ],
    )
    return pl.pallas_call(
        project_kernel,
        grid_spec=spec,
        out_shape=[
            jax.ShapeDtypeStruct((4, tokens, 960), jnp.bfloat16),
            jax.ShapeDtypeStruct((width, 1280), jnp.bfloat16),
        ],
        compiler_params=pltpu.CompilerParams(vmem_limit_bytes=48 << 20),
        cost_estimate=pl.CostEstimate(flops=24_000_000_000, bytes_accessed=35_000_000, transcendentals=0),
        name="project",
    )(shard, x, weights, bias)


def frame_kernel(shard_ref, near_own, near_other, far_own, far_other, w_ref, fold_ref, out_ref, sums_ref):
    @pl.when(pl.program_id(0) == 0)
    def _():
        sums_ref[...] = jnp.zeros_like(sums_ref)

    total = None
    for p, back_ref in enumerate((near_own, near_other, far_own, far_other)):
        back = back_ref[...]
        piece = dot(back, w_ref[p ^ shard_ref[0]][:, :960], NT)
        total = piece if total is None else total + piece
        sums_ref[p] += jnp.sum(back.astype(jnp.float32), axis=0, keepdims=True)
    total = total.astype(jnp.bfloat16)
    for row in range(out_ref.shape[0]):
        piece = total[row * 80:(row + 1) * 80, :]
        out_ref[row] = dot(fold_ref[...], piece, NN).astype(jnp.bfloat16)


def frame_back(shard, backs, weights, fold):
    width = weights.shape[1]
    chunk = 7
    back_spec = pl.BlockSpec((chunk * 80, 960), lambda g, s: (g, 0))
    spec = pltpu.PrefetchScalarGridSpec(
        num_scalar_prefetch=1,
        grid=(28 // chunk,),
        in_specs=[back_spec] * 4 + [
            pl.BlockSpec((4, width, 1280), lambda g, s: (0, 0, 0), pipeline_mode=pl.Buffered(1)),
            pl.BlockSpec(fold.shape, lambda g, s: (0, 0)),
        ],
        out_specs=[
            pl.BlockSpec((chunk, 64, width), lambda g, s: (g, 0, 0)),
            pl.BlockSpec((4, 1, 960), lambda g, s: (0, 0, 0)),
        ],
    )
    return pl.pallas_call(
        frame_kernel,
        grid_spec=spec,
        out_shape=[
            jax.ShapeDtypeStruct((28, 64, width), jnp.bfloat16),
            jax.ShapeDtypeStruct((4, 1, 960), jnp.float32),
        ],
        compiler_params=pltpu.CompilerParams(vmem_limit_bytes=58 << 20),
        cost_estimate=pl.CostEstimate(flops=1_000_000, bytes_accessed=1_000_000, transcendentals=0),
        name="frame_back",
    )(shard, *backs, weights, fold)


def turn_kernel(x_ref, out_ref):
    out_ref[...] = x_ref[...].T


def turn(x):
    return pl.pallas_call(
        turn_kernel,
        out_shape=jax.ShapeDtypeStruct(x.shape[::-1], x.dtype),
        compiler_params=pltpu.CompilerParams(vmem_limit_bytes=48 << 20),
        cost_estimate=pl.CostEstimate(flops=0, bytes_accessed=12_000_000, transcendentals=0),
        name="turn",
    )(x)


ROWS = 16
FRAME = 28
EARLY, LATE = 6, 12
EPSILON = 1e-06


def swap(values, shifts):
    return lax.ppermute(values, "tensor", shifts)


def own(values, index, axis=0):
    return lax.dynamic_index_in_dim(values, index, axis, keepdims=False)


def gather_small(values, shard):
    parts = [values]
    for step in (1, 2, 3):
        parts.append(swap(values, [(i, (i + step) % 4) for i in range(4)]))
    stack = jnp.stack(parts)
    return jnp.stack([own(stack, (shard - i) % 4) for i in range(4)])


CORES = [(0, 1), (1, 0), (2, 3), (3, 2)]
SIDES = [(0, 2), (2, 0), (1, 3), (3, 1)]


def add_low(left, right):
    return (left.astype(jnp.float32) + right.astype(jnp.float32)).astype(jnp.bfloat16)


def scatter_dp(quarter):
    return lax.psum_scatter(quarter, "dp", scatter_dimension=0, tiled=True)


def after(first, *values):
    return lax.optimization_barrier((first,) + values)[1:]


def sum_everywhere(values):
    values = values + swap(values, CORES)
    values = values + swap(values, SIDES)
    count = lax.axis_size("dp")
    step = 1
    while step < count:
        values = values + lax.ppermute(values, "dp", [(i, i ^ step) for i in range(count)])
        step *= 2
    return values


def statistics(values):
    average = jnp.mean(values, axis=-1, keepdims=True)
    centred = values - average
    rstd = lax.rsqrt(jnp.mean(centred * centred, axis=-1, keepdims=True) + EPSILON)
    return centred * rstd, rstd


def norm_back(grad, gain, hat, rstd):
    scaled = grad * gain
    mean_one = jnp.mean(scaled, axis=-1, keepdims=True)
    mean_two = jnp.mean(scaled * hat, axis=-1, keepdims=True)
    return rstd * (scaled - mean_one - hat * mean_two)


def column_selector():
    column = np.arange(GRID)
    place = SIDE * (column // WIN) + column % WIN
    select = np.zeros((NWIN * SIDE, GRID), np.float32)
    select[place, column] = 1.0
    return jnp.asarray(select, jnp.bfloat16)


def fast_shards(
    inputs,
    cotangent,
    teacher,
    qkv_weight,
    proj_weight,
    up_weight,
    down_weight,
    qv_bias,
    up_bias,
    norm_gains,
    norm_shifts,
    out_biases,
    rel_tables,
):
    f32, bf16 = jnp.float32, jnp.bfloat16
    shard = lax.axis_index("tensor")
    both = ("tensor", "dp")
    tokens = ROWS * GRID
    inner = qkv_weight.shape[1]
    joint = jnp.concatenate([qkv_weight.transpose(1, 0, 2).reshape(inner, 960), proj_weight.T], axis=1)
    joint = jnp.concatenate([joint, up_weight], axis=1)
    joint_all = lax.all_gather(joint, both, axis=0, tiled=True).reshape(4, D, 2560)
    biases = gather_small(jnp.concatenate([qv_bias.reshape(-1), up_bias]), shard)
    qkv_bias = jnp.concatenate(
        [biases[:, :320], jnp.zeros((4, 320), bf16), biases[:, 320:640]], axis=1
    ).astype(f32)
    up_bias_all = biases[:, 640:].astype(f32)

    gains = norm_gains.astype(f32)
    shifts = norm_shifts.astype(f32)
    image = inputs[0]
    above = swap(image[ROWS - EARLY:], [(i, i + 1) for i in range(3)])
    below = swap(image[:LATE], [(i + 1, i) for i in range(3)])
    framed = lax.dynamic_slice_in_dim(
        jnp.concatenate([above, image, below]), EARLY - 2 * shard, FRAME, 0
    )
    frame_hat, _ = statistics(framed.astype(f32))
    inside = (WIN * shard + jnp.arange(FRAME) < GRID)[:, None, None]
    normed = jnp.where(inside, frame_hat * gains[0] + shifts[0], 0.0).astype(bf16)
    select = column_selector()
    windows = jnp.einsum("pc,rcd->rpd", select, normed, preferred_element_type=f32).astype(bf16)
    flat = windows.reshape(FRAME * NWIN * SIDE, D)
    where = shard[None].astype(jnp.int32)
    qkv, proj_full = project(where, flat, joint_all, qkv_bias[:, None, :])
    qkv = qkv.reshape(4, FRAME, NWIN * SIDE, 960)
    tables, back_tables = bias_tables(rel_tables)
    select_keys, spread_keys = selectors()
    flat_turned = turn(flat)
    (down_shard,) = after((joint_all, flat_turned), down_weight.T)
    down_all = lax.all_gather(down_shard, both, axis=0, tiled=True).reshape(4, D, 1280)
    up_all = joint_all[:, :, 1280:]
    attended = window_attend(where, qkv, tables, select_keys)
    attended = jnp.einsum("pc,rpd->rcd", select, attended, preferred_element_type=f32)
    attended = attended.astype(bf16).reshape(tokens, D)

    source = image.astype(f32).reshape(tokens, D)
    branch = jnp.einsum("nk,ck->nc", attended, proj_full, preferred_element_type=f32)
    middle = source + branch + out_biases[0].astype(f32)
    second_hat, second_rstd = statistics(middle)
    normed_two = (second_hat * gains[1] + shifts[1]).astype(bf16)
    hidden = jnp.einsum("nd,tdm->tnm", normed_two, up_all, preferred_element_type=f32)
    hidden = hidden + up_bias_all[:, None, :]
    cdf = 0.5 + 0.5 * lax.erf(hidden * (0.5 ** 0.5))
    active = (hidden * cdf).astype(bf16)
    slope = (cdf + hidden * (jnp.exp(-0.5 * hidden * hidden) * (0.5 / np.pi) ** 0.5)).astype(bf16)
    result = jnp.einsum("tnm,tcm->nc", active, down_all, preferred_element_type=f32)
    result = middle + result + out_biases[1].astype(f32)
    mismatch = result - teacher[0].astype(f32).reshape(tokens, D)
    loss_total = jnp.sum(mismatch * mismatch)
    output = result.astype(bf16)

    result_grad = cotangent[0].astype(f32).reshape(tokens, D) + mismatch
    result_low = result_grad.astype(bf16)
    def down_block(p):
        return jnp.einsum("nc,nm->cm", result_low, own(active, shard ^ p), preferred_element_type=f32)

    sends = [down_block(3).astype(bf16), down_block(1).astype(bf16)]
    down_three, down_one = swap(sends[0], CORES), swap(sends[1], CORES)
    (result_next,) = after(tuple(sends), result_low)
    active_grad = jnp.einsum("nc,tcm->tnm", result_next, down_all, preferred_element_type=f32)
    hidden_grad = active_grad * slope.astype(f32)
    up_bias_acc = jnp.sum(hidden_grad, axis=1)
    hidden_low = hidden_grad.astype(bf16)
    down_far = (down_block(2) + down_three.astype(f32)).astype(bf16)
    down_near = (down_block(0) + down_one.astype(f32)).astype(bf16)
    down_side = swap(down_far, SIDES)
    hidden_low, normed_two = after((down_far, down_near), hidden_low, normed_two)

    def up_block(p):
        return jnp.einsum("nd,nm->dm", normed_two, own(hidden_low, shard ^ p), preferred_element_type=f32)

    sends = [up_block(3).astype(bf16), up_block(1).astype(bf16)]
    up_three, up_one = swap(sends[0], CORES), swap(sends[1], CORES)
    (hidden_next,) = after(tuple(sends), hidden_low)
    second_grad = jnp.einsum("tnm,tdm->nd", hidden_next, up_all, preferred_element_type=f32)
    middle_grad = result_grad + norm_back(second_grad, gains[1], second_hat, second_rstd)
    second_gain = jnp.sum(second_grad * second_hat, axis=0)
    second_shift = jnp.sum(second_grad, axis=0)
    middle_low = middle_grad.astype(bf16)
    attended_grad = jnp.einsum("nc,ck->nk", middle_low, proj_full, preferred_element_type=f32)
    attended_grad = attended_grad.astype(bf16).reshape(ROWS, GRID, D)
    attended_grad = jnp.einsum("pc,rcd->rpd", select, attended_grad, preferred_element_type=f32)
    attended_grad = attended_grad.astype(bf16)
    up_far = (up_block(2) + up_three.astype(f32)).astype(bf16)
    up_near = (up_block(0) + up_one.astype(f32)).astype(bf16)
    up_side = swap(up_far, SIDES)

    def proj_block(p):
        part = attended[:, 320 * p:320 * p + 320]
        return jnp.einsum("nc,nk->ck", middle_low, part, preferred_element_type=f32)

    proj_sends = (proj_block(3).astype(bf16), proj_block(1).astype(bf16))
    proj_three, proj_one = swap(proj_sends[0], CORES), swap(proj_sends[1], CORES)
    (down_near,) = after((up_far, up_near, proj_sends), down_near)
    down_quarter = add_low(down_near, down_side)
    (grad_far,) = after((up_far, up_near, down_quarter), attended_grad)
    far_own, far_other, far_sums = window_attend_back(
        1, where, qkv, grad_far, tables, back_tables, select_keys, spread_keys
    )

    def flatten(back):
        return back.reshape(FRAME * NWIN * SIDE, 960)

    def qkv_block(tokens_in, back):
        return jnp.einsum("dn,nc->dc", tokens_in, back, preferred_element_type=f32)

    far_own, far_other = flatten(far_own), flatten(far_other)
    qkv_send = qkv_block(flat_turned, far_other).astype(bf16)
    qkv_three = swap(qkv_send, CORES)
    flat_far, up_side, down_grad, _ = lax.optimization_barrier(
        (flat_turned, up_side, scatter_dp(down_quarter), qkv_send)
    )
    up_quarter = add_low(up_near, up_side)
    proj_far = (proj_block(2) + proj_three.astype(f32)).astype(bf16)
    proj_near = (proj_block(0) + proj_one.astype(f32)).astype(bf16)
    qkv_far = (qkv_block(flat_far, far_own) + qkv_three.astype(f32)).astype(bf16)
    joint_far = jnp.concatenate([qkv_far, proj_far], axis=1)
    joint_far, proj_near, up_quarter, grad_near = lax.optimization_barrier(
        (joint_far, proj_near, up_quarter, attended_grad)
    )
    far_side = swap(joint_far, SIDES)
    near_own, near_other, near_sums = window_attend_back(
        0, where, qkv, grad_near, tables, back_tables, select_keys, spread_keys
    )
    near_own, near_other = flatten(near_own), flatten(near_other)
    qkv_send = qkv_block(flat_turned, near_other).astype(bf16)
    qkv_one = swap(qkv_send, CORES)
    backs = after(qkv_send, near_own, near_other, far_own, far_other)
    frame_grad, bias_sums = frame_back(where, backs, joint_all, select.T)
    spread = jnp.zeros((EARLY + ROWS + LATE, GRID, D), bf16)
    spread = lax.dynamic_update_slice_in_dim(spread, frame_grad, EARLY - 2 * shard, 0)
    flat_near, far_side, spread = lax.optimization_barrier((flat_turned, far_side, spread))
    qkv_near = qkv_block(flat_near, near_own) + qkv_one.astype(f32)
    near = jnp.concatenate([qkv_near.astype(bf16), proj_near], axis=1)
    joint_quarter = add_low(near, far_side)
    up_grad, joint_quarter = lax.optimization_barrier((scatter_dp(up_quarter), joint_quarter))
    joint_grad = scatter_dp(joint_quarter)
    table_sums = far_sums + near_sums
    bias_sums = bias_sums[:, 0]
    qv_acc = jnp.stack([bias_sums[:, :320], bias_sums[:, 640:]], axis=1)
    qv_acc = jnp.stack([own(qv_acc, shard ^ t) for t in range(4)])
    table_sums = table_sums[:, :320].reshape(2, GROUP, 32, GROUP, HEAD_DIM)
    table_acc = jnp.einsum("phrhd->prd", table_sums)
    table_acc = jnp.stack([table_acc[0, :27][::-1], table_acc[1, :27]])
    from_next = swap(spread[:EARLY], [(i + 1, i) for i in range(3)])
    from_before = swap(spread[EARLY + ROWS:], [(i, i + 1) for i in range(3)])
    first_grad = spread[EARLY:EARLY + ROWS].astype(f32)
    first_grad = first_grad + jnp.pad(from_next.astype(f32), ((ROWS - EARLY, 0), (0, 0), (0, 0)))
    first_grad = first_grad + jnp.pad(from_before.astype(f32), ((0, ROWS - LATE), (0, 0), (0, 0)))
    first_grad = first_grad.reshape(tokens, D)
    first_hat, first_rstd = statistics(source)
    first_gain = jnp.sum(first_grad * first_hat, axis=0)
    first_shift = jnp.sum(first_grad, axis=0)
    input_grad = middle_grad + norm_back(first_grad, gains[0], first_hat, first_rstd)

    small = [
        qv_acc, up_bias_acc, first_gain, second_gain, first_shift, second_shift,
        jnp.sum(middle_grad, axis=0), jnp.sum(result_grad, axis=0), table_acc, loss_total,
    ]
    sums = sum_everywhere(jnp.concatenate([part.reshape(-1) for part in small]))
    parts = []
    place = 0
    for part in small:
        parts.append(sums[place:place + part.size].reshape(part.shape))
        place += part.size
    qv_sum, up_sum, gain_one, gain_two, shift_one, shift_two, bias_one, bias_two, table_grad, loss_sum = parts
    loss = loss_sum / (tokens * D * lax.axis_size("dp") * lax.axis_size("tensor"))
    return (
        output.reshape(1, ROWS, GRID, D),
        input_grad.reshape(1, ROWS, GRID, D),
        loss,
        joint_grad[:, :960].reshape(inner, 3, 320).transpose(1, 0, 2).astype(f32),
        joint_grad[:, 960:].T.astype(f32),
        up_grad.astype(f32),
        down_grad.T.astype(f32),
        own(qv_sum, shard),
        own(up_sum, shard),
        jnp.stack([gain_one, gain_two]),
        jnp.stack([shift_one, shift_two]),
        jnp.stack([bias_one, bias_two]),
        table_grad,
    )


def solution(mesh):
    in_specs = (
        P("dp", "tensor", None, None),
        P("dp", "tensor", None, None),
        P("dp", "tensor", None, None),
        P(None, "dp", "tensor"),
        P("tensor", "dp"),
        P("dp", "tensor"),
        P("tensor", "dp"),
        P(None, "tensor"),
        P("tensor"),
        P(),
        P(),
        P(),
        P(),
    )
    out_specs = (
        P("dp", "tensor", None, None),
        P("dp", "tensor", None, None),
        P(),
        P(None, "dp", "tensor"),
        P("tensor", "dp"),
        P("dp", "tensor"),
        P("tensor", "dp"),
        P(None, "tensor"),
        P("tensor"),
        P(),
        P(),
        P(),
        P(),
    )
    fits = mesh.shape["tensor"] == 4 and GRID // mesh.shape["tensor"] == 16
    shards = fast_shards if fits else general_shards
    return jax.shard_map(shards, mesh=mesh, in_specs=in_specs, out_specs=out_specs, check_vma=False)
```
